512 devices in a mesh: tok: 32 (over z, x), vocab: 16 (over y, core).
Axes of the slice: x: 4, y: 8, z: 8, core: 2. Of those that a mesh axis runs over, the one named last changes fastest.
Arguments:
- teacher_hidden: bfloat16 [4096, 4096], P('tok', 'vocab'), may hold values from -6 to 6
- span_table: int32 [4096, 2], P('tok'), may hold values from 0 to 4096, as said below
- target_ids: int32 [4096], P('tok'), may hold values from 0 to 65535
- student_logits: bfloat16 [4096, 65536], P('tok', 'vocab')
- proj_weight: bfloat16 [1536, 4096], P('vocab')
- norm_gain: float32 [1536], replicated, may hold values from 0.1 to 1.9
- head_weight: bfloat16 [65536, 1536], P(('vocab', 'tok'))
Outputs:
- token_loss: float32 [4096], P('tok')
- proj_grad: float32 [1536, 4096], P('vocab', 'tok')
The draws below stay inside these ranges and needn't reach their ends.
Inputs may be any that keep to these rules, and one draw needn't show every extreme that they name: `span_table`: 1 <= end - start <= 4 for every row; for the tokens of aligned block k of 128 rows, start >= k * 128 - 128 // 4 and end <= (k + 1) * 128 + 128 // 4, both reached in every block that does not touch the end of the trace.
All inputs are finite; a program needn't handle non-finite values.
Results may differ from the reference program's by a relative error of at most 0.0062.
Values may be sent and summed in bfloat16 or wider, within the bound.
A program may use at most 64 MiB of HBM per device.

```python
import math
import jax
import jax.numpy as jnp
import numpy as np
from jax import lax

DT = 4096
DS = 1536
TOK_DEV = 128
TOKENS = 4096
VOCAB = 65536
N_TOK = 32


def draw_span_table(key, part):
    margin = TOK_DEV // 4
    key_drift, key_left, key_right = jax.random.split(jax.random.fold_in(key, 11), 3)
    tokens = jnp.arange(TOKENS, dtype=jnp.int32)
    local = tokens % TOK_DEV
    drift = jax.random.randint(key_drift, (TOKENS,), -(margin - 1), margin, dtype=jnp.int32)
    left = jax.random.randint(key_left, (TOKENS,), 0, 2, dtype=jnp.int32)
    right = jax.random.randint(key_right, (TOKENS,), 0, 3, dtype=jnp.int32)
    drift = jnp.where(local == 0, -(margin - 1), drift)
    left = jnp.where(local == 0, 1, left)
    drift = jnp.where(local == TOK_DEV - 1, margin - 1, drift)
    right = jnp.where(local == TOK_DEV - 1, 1, right)
    center = jnp.clip(tokens + drift, 0, TOKENS - 1)
    starts = jnp.maximum(center - left, 0)
    ends = jnp.minimum(center + 1 + right, TOKENS)
    return jnp.stack([starts, ends], axis=1).astype(jnp.int32)


def draw_student_logits(key, part):
    key_base, key_rows, key_cols = jax.random.split(jax.random.fold_in(key, 23), 3)
    base = jnp.clip(jax.random.normal(key_base, (TOKENS, VOCAB), jnp.float32), -6.0, 6.0)
    rows = jnp.exp(jax.random.uniform(key_rows, (TOKENS, 1), jnp.float32, math.log(0.1), math.log(5.0)))
    cols = jnp.exp(jax.random.uniform(key_cols, (1, VOCAB), jnp.float32, math.log(0.6), math.log(1.8)))
    values = base * rows * cols
    return values.astype(jnp.bfloat16)


def draw_proj_weight(key, part):
    key_base, key_rows = jax.random.split(jax.random.fold_in(key, 37), 2)
    base = jnp.clip(jax.random.normal(key_base, (DS, DT), jnp.float32), -6.0, 6.0)
    order = jnp.arange(DS, dtype=jnp.float32)[:, None] / DS
    jitter = jnp.exp(jax.random.uniform(key_rows, (DS, 1), jnp.float32, math.log(0.8), math.log(1.25)))
    rising = jnp.power(10.0, order)
    return (base * rising * jitter * DT ** (-0.5)).astype(jnp.bfloat16)


def draw_head_weight(key, part):
    key_base, key_rows, key_shared = jax.random.split(jax.random.fold_in(key, 53), 3)
    base = jnp.clip(jax.random.normal(key_base, (VOCAB, DS), jnp.float32), -6.0, 6.0)
    rows = jnp.exp(jax.random.uniform(key_rows, (VOCAB, 1), jnp.float32, math.log(0.6), math.log(1.6)))
    values = base * rows * (3.0 * DS ** (-0.5))
    shared = jnp.clip(jax.random.normal(key_shared, (1, DS), jnp.float32), -6.0, 6.0) * (3.0 * DS ** (-0.5))
    values = values + shared
    return values.astype(jnp.bfloat16)


def with_ends(values, stream_key, smallest, high):
    extent = values.shape
    spot = [jax.random.randint(jax.random.fold_in(stream_key, axis), (), 0, extent[axis]) for axis in range(len(extent))]
    values = values.at[tuple(spot)].set(smallest)
    longest = extent.index(max(extent))
    spot[longest] = (spot[longest] + 1) % extent[longest]
    return values.at[tuple(spot)].set(high)


def level_of(stream_key, dims, pieces, low, high):
    gain, own = 1.0, jax.random.fold_in(stream_key, 6)
    for dim, parts in pieces:
        draws = jnp.exp(jax.random.uniform(jax.random.fold_in(own, dim), (parts,), jnp.float32, low / len(pieces), high / len(pieces)))
        gain = gain * jnp.repeat(draws, dims[dim] // parts).reshape([-1 if axis == dim else 1 for axis in range(len(dims))])
    return gain


def cumulative_ranks(count, slope):
    weights = [(1 << 20) // math.isqrt(grade ** slope) + 1 for grade in range(1, count + 1)]
    deviation = 1 + sum(weights) // (1 << 30)
    return np.cumsum(np.array([max(1, weight // deviation) for weight in weights]))


def ranked_ids(key, shape, number_of, slope):
    listing = cumulative_ranks(number_of, slope)
    pick = jax.random.randint(jax.random.fold_in(key, 1), shape, 0, int(listing[number_of - 1]))
    standing = jnp.searchsorted(jnp.asarray(listing, jnp.int32), pick, side="right")
    return jax.random.permutation(jax.random.fold_in(key, 2), number_of)[standing].astype(jnp.int32)


def scatter_about(stream_key, dims, width, limit, pieces=(), kind=jnp.bfloat16):
    gain = level_of(stream_key, dims, pieces, -0.22, 0.18) if pieces else 1.0
    drawn = jax.random.normal(stream_key, dims, jnp.float32) * width * gain
    return jnp.minimum(jnp.maximum(drawn, -limit), limit).astype(kind)


def setup_inputs(seed: int = 0) -> dict:
    arg_keys = jax.random.split(jax.random.key(seed), 8)
    teacher_hidden = scatter_about(arg_keys[0], (TOKENS, DT), 1.0, 6.0, ((0, 32), (1, 16)))
    span_table = draw_span_table(jax.random.fold_in(arg_keys[7], 71), 0)
    target_ids = with_ends(ranked_ids(arg_keys[2], (TOKENS,), VOCAB, 2), jax.random.fold_in(arg_keys[2], 3), 0, VOCAB - 1).astype(jnp.int32)
    student_logits = draw_student_logits(jax.random.fold_in(arg_keys[7], 71), 0)
    proj_weight = draw_proj_weight(jax.random.fold_in(arg_keys[7], 71), 0)
    norm_gain = jnp.clip(1.0 + 0.18 * jax.random.normal(arg_keys[5], (DS,), jnp.float32), 0.1, 1.9)
    head_weight = draw_head_weight(jax.random.fold_in(arg_keys[7], 71), 0)
    return {"teacher_hidden": teacher_hidden, "span_table": span_table, "target_ids": target_ids, "student_logits": student_logits, "proj_weight": proj_weight, "norm_gain": norm_gain, "head_weight": head_weight}


EPS = 1e-06

def reference(teacher_hidden, span_table, target_ids, student_logits, proj_weight, norm_gain, head_weight):
    margin = TOK_DEV // 4
    padded = jnp.pad(teacher_hidden, ((margin, margin), (0, 0)))

    def pool_block(block):
        first = (block * TOK_DEV).astype(jnp.int32)
        extended = lax.dynamic_slice_in_dim(padded, first, TOK_DEV + 2 * margin, 0)
        spans = lax.dynamic_slice_in_dim(span_table, first, TOK_DEV, 0)
        positions = first - margin + jnp.arange(TOK_DEV + 2 * margin, dtype=jnp.int32)
        member = ((positions[None, :] >= spans[:, 0:1]) & (positions[None, :] < spans[:, 1:2])).astype(jnp.bfloat16)
        summed = jnp.dot(member, extended, preferred_element_type=jnp.float32)
        counts = (spans[:, 1] - spans[:, 0]).astype(jnp.float32)
        return (summed / counts[:, None]).astype(jnp.bfloat16)
    pooled = lax.map(pool_block, jnp.arange(N_TOK, dtype=jnp.int32)).reshape(TOKENS, DT)
    projected = jnp.dot(pooled, proj_weight.T, preferred_element_type=jnp.float32)
    inverse = lax.rsqrt(lax.optimization_barrier(jnp.mean(projected * projected, axis=1)) + EPS)
    scaled = projected * inverse[:, None]
    normed = (scaled * norm_gain).astype(jnp.bfloat16)

    def head_block(block):
        first = (block * TOK_DEV).astype(jnp.int32)
        normed_rows = lax.dynamic_slice_in_dim(normed, first, TOK_DEV, 0)
        student = lax.dynamic_slice_in_dim(student_logits, first, TOK_DEV, 0).astype(jnp.float32)
        targets = lax.dynamic_slice_in_dim(target_ids, first, TOK_DEV, 0)
        head_logits = jnp.dot(normed_rows, head_weight.T, preferred_element_type=jnp.float32)
        student_top = lax.optimization_barrier(jnp.max(student, axis=1))
        student_lse = student_top + jnp.log(lax.optimization_barrier(jnp.sum(jnp.exp(student - student_top[:, None]), axis=1)))
        head_top = lax.optimization_barrier(jnp.max(head_logits, axis=1))
        head_lse = head_top + jnp.log(lax.optimization_barrier(jnp.sum(jnp.exp(head_logits - head_top[:, None]), axis=1)))
        log_student = student - student_lse[:, None]
        log_head = head_logits - head_lse[:, None]
        prob_student = jnp.exp(log_student)
        prob_head = jnp.exp(log_head)
        vocab_ids = jnp.arange(VOCAB, dtype=jnp.int32)
        hit = (vocab_ids[None, :] == targets[:, None]).astype(jnp.float32)
        divergence = lax.optimization_barrier(jnp.sum(prob_student * (log_student - log_head), axis=1))
        picked = lax.optimization_barrier(jnp.sum(hit * head_logits, axis=1))
        loss = divergence + head_lse - picked
        logit_grad = (2.0 * prob_head - prob_student - hit).astype(jnp.bfloat16)
        normed_grad = jnp.dot(logit_grad, head_weight, preferred_element_type=jnp.float32)
        return (loss, normed_grad)
    losses, normed_grads = lax.map(head_block, jnp.arange(N_TOK, dtype=jnp.int32))
    token_loss = losses.reshape(TOKENS)
    normed_grad = normed_grads.reshape(TOKENS, DS)
    gain_grad = normed_grad * norm_gain
    inner = lax.optimization_barrier(jnp.sum(gain_grad * scaled, axis=1))
    out_grad = (inverse[:, None] * (gain_grad - scaled * inner[:, None] / DS)).astype(jnp.bfloat16)
    proj_grad = jnp.dot(out_grad.T, pooled, preferred_element_type=jnp.float32)
    return (token_loss, proj_grad)
```

```python
import functools

import jax
import jax.numpy as jnp
from jax import lax
from jax.experimental import pallas as pl
from jax.experimental.pallas import tpu as pltpu
from jax.sharding import PartitionSpec as P

EPS = 1e-06
MESH = pl.DeviceIdType.MESH


def greet(peers):
    barrier = pltpu.get_barrier_semaphore()
    for peer in peers:
        pl.semaphore_signal(barrier, inc=1, device_id={"vocab": peer}, device_id_type=MESH)
    pl.semaphore_wait(barrier, len(peers))


def gather_kernel(chips, block, out, send, recv, pass_send, pass_recv, keep):
    me = lax.axis_index("vocab")
    core = lax.rem(me, 2)
    chip = lax.div(me, 2)
    partner = chip * 2 + (1 - core)
    ahead = [lax.rem(chip + step, chips) * 2 + core for step in range(1, chips)]
    behind = [lax.rem(chip + chips - step, chips) * 2 + core for step in range(1, chips)]
    greet(ahead + [partner])
    steps = sorted(range(1, chips), key=lambda step: -min(step, chips - step))
    copies = {}
    for step in steps:
        copies[step] = pltpu.make_async_remote_copy(
            src_ref=block, dst_ref=out.at[me], send_sem=send.at[step], recv_sem=recv.at[step],
            device_id={"vocab": ahead[step - 1]}, device_id_type=MESH,
        )
        copies[step].start()
    own = pltpu.make_async_copy(block, out.at[me], keep)
    own.start()
    passes = [
        pltpu.make_async_remote_copy(
            src_ref=block, dst_ref=out.at[me], send_sem=pass_send.at[0], recv_sem=pass_recv.at[0],
            device_id={"vocab": partner}, device_id_type=MESH,
        )
    ]
    passes[0].start()
    for step in reversed(steps):
        copies[step].wait_recv()
        source = behind[step - 1]
        onward = pltpu.make_async_remote_copy(
            src_ref=out.at[source], dst_ref=out.at[source],
            send_sem=pass_send.at[step], recv_sem=pass_recv.at[step],
            device_id={"vocab": partner}, device_id_type=MESH,
        )
        onward.start()
        passes.append(onward)
    for onward in passes:
        onward.wait()
    for step in steps:
        copies[step].wait_send()
    own.wait()


def vocab_gather(block, collective_id):
    count = lax.axis_size("vocab")
    chips = count // 2
    return pl.pallas_call(
        functools.partial(gather_kernel, chips),
        out_shape=jax.ShapeDtypeStruct((count,) + block.shape, block.dtype),
        in_specs=[pl.BlockSpec(memory_space=pltpu.VMEM)],
        out_specs=pl.BlockSpec(memory_space=pltpu.VMEM),
        scratch_shapes=[pltpu.SemaphoreType.DMA((chips,))] * 4 + [pltpu.SemaphoreType.DMA],
        compiler_params=pltpu.CompilerParams(collective_id=collective_id, has_side_effects=True),
        cost_estimate=pl.CostEstimate(flops=0, bytes_accessed=30_000_000, transcendentals=0),
    )(block)


def exchange_kernel(count, blocks, out, send, recv, keep):
    me = lax.axis_index("vocab")
    ahead = [lax.rem(me + step, count) for step in range(1, count)]
    greet(ahead)
    own = pltpu.make_async_copy(blocks.at[me], out.at[me], keep)
    own.start()
    copies = []
    for step in sorted(range(1, count), key=lambda step: -min(step, count - step)):
        copy = pltpu.make_async_remote_copy(
            src_ref=blocks.at[ahead[step - 1]], dst_ref=out.at[me],
            send_sem=send.at[step], recv_sem=recv.at[step],
            device_id={"vocab": ahead[step - 1]}, device_id_type=MESH,
        )
        copy.start()
        copies.append(copy)
    for copy in copies:
        copy.wait()
    own.wait()


def vocab_exchange(blocks, collective_id):
    count = lax.axis_size("vocab")
    return pl.pallas_call(
        functools.partial(exchange_kernel, count),
        out_shape=jax.ShapeDtypeStruct(blocks.shape, blocks.dtype),
        in_specs=[pl.BlockSpec(memory_space=pltpu.VMEM)],
        out_specs=pl.BlockSpec(memory_space=pltpu.VMEM),
        scratch_shapes=[pltpu.SemaphoreType.DMA((count,))] * 2 + [pltpu.SemaphoreType.DMA],
        compiler_params=pltpu.CompilerParams(collective_id=collective_id, has_side_effects=True),
        cost_estimate=pl.CostEstimate(flops=0, bytes_accessed=30_000_000, transcendentals=0),
    )(blocks)


def padded(cells, axis, width):
    count = lax.axis_size(axis)
    ends = count - 1
    head = cells[:width]
    tail = cells[cells.shape[0] - width :]
    return jnp.concatenate(
        [
            lax.ppermute(tail, axis, [(i, (i + 1) % count) for i in range(ends)]),
            cells,
            lax.ppermute(head, axis, [((i + 1) % count, i) for i in range(ends)]),
        ],
        axis=0,
    )


def on_device(
    teacher_hidden, span_table, target_ids, student_logits, proj_weight, norm_gain, head_weight
):
    n_tok = lax.axis_size("tok")
    n_vocab = lax.axis_size("vocab")
    head_full = lax.all_gather(head_weight, "tok", axis=0, tiled=True)
    rows = teacher_hidden.shape[0]
    margin = rows // 4
    extended = padded(teacher_hidden, "tok", margin)
    first_row = lax.axis_index("tok") * rows - margin
    positions = first_row + jnp.arange(rows + 2 * margin, dtype=jnp.int32)
    starts = span_table[:, 0]
    ends = span_table[:, 1]
    member = (
        (positions[None, :] >= starts[:, None]) & (positions[None, :] < ends[:, None])
    ).astype(jnp.bfloat16)
    summed = jnp.dot(member, extended, preferred_element_type=jnp.float32)
    counts = (ends - starts).astype(jnp.float32)
    pooled_part = (summed / counts[:, None]).astype(jnp.bfloat16)
    part = pooled_part.shape[1]
    pooled = vocab_gather(pooled_part, 0)
    pooled = jnp.swapaxes(pooled, 0, 1).reshape(rows, n_vocab * part)
    projected_part = lax.dot_general(
        proj_weight, pooled, (((1,), (1,)), ((), ())), preferred_element_type=jnp.float32
    )
    width_part = proj_weight.shape[0]
    width = norm_gain.shape[0]
    projected = vocab_gather(projected_part, 1).reshape(width, rows)
    inverse = lax.rsqrt(jnp.sum(projected * projected, axis=0) / width + EPS)
    normed = (projected * inverse[None, :] * norm_gain[:, None]).astype(jnp.bfloat16)
    column_part = n_vocab * part // n_tok
    pooled_columns = lax.all_to_all(
        pooled.reshape(rows, n_tok, column_part), "tok", 1, 0, tiled=True
    ).reshape(n_tok * rows, column_part)

    student = student_logits.astype(jnp.float32)
    head_logits = lax.dot_general(
        normed, head_full, (((0,), (1,)), ((), ())), preferred_element_type=jnp.float32
    )
    vocab_part = student_logits.shape[1]
    vocab_ids = lax.axis_index("vocab") * vocab_part + jnp.arange(vocab_part, dtype=jnp.int32)
    hit = (vocab_ids[None, :] == target_ids[:, None]).astype(jnp.float32)
    student_top = jnp.max(student, axis=1)
    student_exp = jnp.exp(student - student_top[:, None])
    head_top = jnp.max(head_logits, axis=1)
    head_exp = jnp.exp(head_logits - head_top[:, None])
    stats = jnp.stack(
        [
            student_top,
            jnp.sum(student_exp, axis=1),
            jnp.sum(student_exp * (student - head_logits), axis=1),
            jnp.sum(student_exp * head_logits, axis=1),
            head_top,
            jnp.sum(head_exp, axis=1),
            jnp.sum(head_exp * head_logits, axis=1),
            jnp.sum(hit * head_logits, axis=1),
        ]
    )
    stats = vocab_gather(stats, 2)
    tops = jnp.max(stats, axis=0)
    student_scale = jnp.exp(stats[:, 0] - tops[0])
    head_scale = jnp.exp(stats[:, 4] - tops[4])
    student_total = jnp.sum(stats[:, 1] * student_scale, axis=0)
    student_gap = jnp.sum(stats[:, 2] * student_scale, axis=0) / student_total
    student_head = jnp.sum(stats[:, 3] * student_scale, axis=0) / student_total
    head_total = jnp.sum(stats[:, 5] * head_scale, axis=0)
    head_head = jnp.sum(stats[:, 6] * head_scale, axis=0) / head_total
    picked = jnp.sum(stats[:, 7], axis=0)
    student_lse = tops[0] + jnp.log(student_total)
    head_lse = tops[4] + jnp.log(head_total)
    token_loss = student_gap - student_lse + head_lse + head_lse - picked
    inner = 2.0 * head_head - student_head - picked

    prob_student = jnp.exp(student - student_lse[:, None])
    prob_head = jnp.exp(head_logits - head_lse[:, None])
    logit_grad = (2.0 * prob_head - prob_student - hit).astype(jnp.bfloat16)
    grad_parts = lax.dot_general(
        head_full, logit_grad, (((0,), (1,)), ((), ())), preferred_element_type=jnp.float32
    ).astype(jnp.bfloat16)
    grad_parts = vocab_exchange(grad_parts.reshape(n_vocab, width_part, rows), 3)
    normed_grad = jnp.sum(grad_parts.astype(jnp.float32), axis=0)
    gain_part = lax.dynamic_slice_in_dim(
        norm_gain, lax.axis_index("vocab") * width_part, width_part
    )
    gain_grad = normed_grad * gain_part[:, None]
    scaled_part = projected_part * inverse[None, :]
    out_grad = (inverse[None, :] * (gain_grad - scaled_part * inner[None, :] / width)).astype(
        jnp.bfloat16
    )
    out_grads = lax.all_gather(out_grad, "tok", axis=0)
    out_grads = jnp.swapaxes(out_grads, 0, 1).reshape(width_part, n_tok * rows)
    proj_grad = jnp.dot(out_grads, pooled_columns, preferred_element_type=jnp.float32)
    return (token_loss, proj_grad)


def solution(mesh):
    return jax.shard_map(
        on_device,
        mesh=mesh,
        in_specs=(
            P("tok", "vocab"),
            P("tok", None),
            P("tok"),
            P("tok", "vocab"),
            P("vocab", None),
            P(),
            P(("vocab", "tok"), None),
        ),
        out_specs=(P("tok"), P("vocab", "tok")),
        check_vma=False,
    )
```

```python
import functools

import jax
import jax.numpy as jnp
from jax import lax
from jax.experimental import pallas as pl
from jax.experimental.pallas import tpu as pltpu
from jax.sharding import PartitionSpec as P

EPS = 1e-06
MESH = pl.DeviceIdType.MESH


def greet(peers, tok_peers=()):
    barrier = pltpu.get_barrier_semaphore()
    for peer in peers:
        pl.semaphore_signal(barrier, inc=1, device_id={"vocab": peer}, device_id_type=MESH)
    for peer in tok_peers:
        pl.semaphore_signal(barrier, inc=1, device_id={"tok": peer}, device_id_type=MESH)
    pl.semaphore_wait(barrier, len(peers) + len(tok_peers))


def gather_kernel(chips, block, out, send, recv, pass_send, pass_recv, keep):
    me = lax.axis_index("vocab")
    core = lax.rem(me, 2)
    chip = lax.div(me, 2)
    partner = chip * 2 + (1 - core)
    ahead = [lax.rem(chip + step, chips) * 2 + core for step in range(1, chips)]
    behind = [lax.rem(chip + chips - step, chips) * 2 + core for step in range(1, chips)]
    greet(ahead + [partner])
    steps = sorted(range(1, chips), key=lambda step: -min(step, chips - step))
    copies = {}
    for step in steps:
        copies[step] = pltpu.make_async_remote_copy(
            src_ref=block, dst_ref=out.at[me], send_sem=send.at[step], recv_sem=recv.at[step],
            device_id={"vocab": ahead[step - 1]}, device_id_type=MESH,
        )
        copies[step].start()
    own = pltpu.make_async_copy(block, out.at[me], keep)
    own.start()
    passes = [
        pltpu.make_async_remote_copy(
            src_ref=block, dst_ref=out.at[me], send_sem=pass_send.at[0], recv_sem=pass_recv.at[0],
            device_id={"vocab": partner}, device_id_type=MESH,
        )
    ]
    passes[0].start()
    for step in reversed(steps):
        copies[step].wait_recv()
        source = behind[step - 1]
        onward = pltpu.make_async_remote_copy(
            src_ref=out.at[source], dst_ref=out.at[source],
            send_sem=pass_send.at[step], recv_sem=pass_recv.at[step],
            device_id={"vocab": partner}, device_id_type=MESH,
        )
        onward.start()
        passes.append(onward)
    for onward in passes:
        onward.wait()
    for step in steps:
        copies[step].wait_send()
    own.wait()


def vocab_gather(block, collective_id):
    count = lax.axis_size("vocab")
    chips = count // 2
    return pl.pallas_call(
        functools.partial(gather_kernel, chips),
        out_shape=jax.ShapeDtypeStruct((count,) + block.shape, block.dtype),
        in_specs=[pl.BlockSpec(memory_space=pltpu.VMEM)],
        out_specs=pl.BlockSpec(memory_space=pltpu.VMEM),
        scratch_shapes=[pltpu.SemaphoreType.DMA((chips,))] * 4 + [pltpu.SemaphoreType.DMA],
        compiler_params=pltpu.CompilerParams(collective_id=collective_id, has_side_effects=True),
        cost_estimate=pl.CostEstimate(flops=0, bytes_accessed=30_000_000, transcendentals=0),
    )(block)


def exchange_kernel(
    count, n_tok, blocks, pooled, out, columns, send, recv, tok_send, tok_recv, keep
):
    me = lax.axis_index("vocab")
    row = lax.axis_index("tok")
    ahead = [lax.rem(me + step, count) for step in range(1, count)]
    rows_ahead = [lax.rem(row + step, n_tok) for step in range(1, n_tok)]
    part = columns.shape[2]
    each = pooled.shape[2] // part

    def column_block(index):
        start = pl.multiple_of(lax.rem(index, each) * part, part)
        return pooled.at[lax.div(index, each), :, pl.ds(start, part)]

    greet(ahead, rows_ahead)
    copies = [
        pltpu.make_async_copy(blocks.at[me], out.at[me], keep.at[0]),
        pltpu.make_async_copy(column_block(row), columns.at[row], keep.at[1]),
    ]
    for step in sorted(range(1, count), key=lambda step: -min(step, count - step)):
        copies.append(
            pltpu.make_async_remote_copy(
                src_ref=blocks.at[ahead[step - 1]], dst_ref=out.at[me],
                send_sem=send.at[step], recv_sem=recv.at[step],
                device_id={"vocab": ahead[step - 1]}, device_id_type=MESH,
            )
        )
    for step in range(1, n_tok):
        copies.append(
            pltpu.make_async_remote_copy(
                src_ref=column_block(rows_ahead[step - 1]), dst_ref=columns.at[row],
                send_sem=tok_send.at[step], recv_sem=tok_recv.at[step],
                device_id={"tok": rows_ahead[step - 1]}, device_id_type=MESH,
            )
        )
    for copy in copies:
        copy.start()
    for copy in copies:
        copy.wait()


def exchange(blocks, pooled, collective_id):
    count = lax.axis_size("vocab")
    n_tok = lax.axis_size("tok")
    rows = pooled.shape[1]
    part = pooled.shape[0] * pooled.shape[2] // n_tok
    return pl.pallas_call(
        functools.partial(exchange_kernel, count, n_tok),
        out_shape=(
            jax.ShapeDtypeStruct(blocks.shape, blocks.dtype),
            jax.ShapeDtypeStruct((n_tok, rows, part), pooled.dtype),
        ),
        in_specs=[pl.BlockSpec(memory_space=pltpu.VMEM)] * 2,
        out_specs=[pl.BlockSpec(memory_space=pltpu.VMEM)] * 2,
        scratch_shapes=[pltpu.SemaphoreType.DMA((count,))] * 2
        + [pltpu.SemaphoreType.DMA((n_tok,))] * 2
        + [pltpu.SemaphoreType.DMA((2,))],
        compiler_params=pltpu.CompilerParams(collective_id=collective_id, has_side_effects=True),
        cost_estimate=pl.CostEstimate(flops=0, bytes_accessed=30_000_000, transcendentals=0),
    )(blocks, pooled)


SIDE_X = 4


def tok_gather_kernel(
    n_z, split, block, out, x_send, x_recv, z_send, z_recv, xz_send, xz_recv, zx_send, zx_recv, keep
):
    me = lax.axis_index("tok")
    n_x = SIDE_X
    x = lax.rem(me, n_x)
    z = lax.div(me, n_x)
    x_ahead = [z * n_x + lax.rem(x + step, n_x) for step in range(n_x)]
    x_behind = [z * n_x + lax.rem(x + n_x - step, n_x) for step in range(n_x)]
    z_ahead = [lax.rem(z + step, n_z) * n_x + x for step in range(n_z)]
    z_behind = [lax.rem(z + n_z - step, n_z) * n_x + x for step in range(n_z)]
    greet([], x_ahead[1:] + z_ahead[1:])
    first = pl.ds(0, split)
    second = pl.ds(split, block.shape[0] - split)
    far_first = sorted(range(1, n_z), key=lambda step: -min(step, n_z - step))

    def copy(source, index, rows, send, recv, peer):
        made = pltpu.make_async_remote_copy(
            src_ref=source, dst_ref=out.at[index, rows], send_sem=send, recv_sem=recv,
            device_id={"tok": peer}, device_id_type=MESH,
        )
        made.start()
        return made

    own = pltpu.make_async_copy(block, out.at[me], keep)
    own.start()
    along_x = {
        e: copy(block.at[first], me, first, x_send.at[e], x_recv.at[e], x_ahead[e])
        for e in range(1, n_x)
    }
    along_z = {
        d: copy(block.at[second], me, second, z_send.at[d], z_recv.at[d], z_ahead[d])
        for d in far_first
    }
    later = []

    def onward_z(source, index, e):
        for d in far_first:
            slot = e * n_z + d
            later.append(
                copy(source, index, first, xz_send.at[slot], xz_recv.at[slot], z_ahead[d])
            )

    def onward_x(source, index, d):
        for e in (2, 1, 3):
            slot = d * n_x + e
            later.append(
                copy(source, index, second, zx_send.at[slot], zx_recv.at[slot], x_ahead[e])
            )

    onward_x(block.at[second], me, 0)
    onward_z(block.at[first], me, 0)
    arrivals = [("x", 1), ("x", 3), ("z", 1), ("z", 7), ("x", 2), ("z", 2), ("z", 6)]
    arrivals += [("z", 3), ("z", 5), ("z", 4)]
    for axis, step in arrivals:
        if axis == "x":
            along_x[step].wait_recv()
            onward_z(out.at[x_behind[step], first], x_behind[step], step)
        else:
            along_z[step].wait_recv()
            onward_x(out.at[z_behind[step], second], z_behind[step], step)
    for made in later:
        made.wait()
    for made in list(along_x.values()) + list(along_z.values()):
        made.wait_send()
    own.wait()


def tok_gather(block, collective_id):
    n_tok = lax.axis_size("tok")
    n_z = n_tok // SIDE_X
    return pl.pallas_call(
        functools.partial(tok_gather_kernel, n_z, block.shape[0] // 3),
        out_shape=jax.ShapeDtypeStruct((n_tok,) + block.shape, block.dtype),
        in_specs=[pl.BlockSpec(memory_space=pltpu.VMEM)],
        out_specs=pl.BlockSpec(memory_space=pltpu.VMEM),
        scratch_shapes=[pltpu.SemaphoreType.DMA((SIDE_X,))] * 2
        + [pltpu.SemaphoreType.DMA((n_z,))] * 2
        + [pltpu.SemaphoreType.DMA((n_tok,))] * 4
        + [pltpu.SemaphoreType.DMA],
        compiler_params=pltpu.CompilerParams(collective_id=collective_id, has_side_effects=True),
        cost_estimate=pl.CostEstimate(flops=0, bytes_accessed=30_000_000, transcendentals=0),
    )(block)


def padded(cells, axis, width):
    count = lax.axis_size(axis)
    ends = count - 1
    head = cells[:width]
    tail = cells[cells.shape[0] - width :]
    return jnp.concatenate(
        [
            lax.ppermute(tail, axis, [(i, (i + 1) % count) for i in range(ends)]),
            cells,
            lax.ppermute(head, axis, [((i + 1) % count, i) for i in range(ends)]),
        ],
        axis=0,
    )


def on_device(
    teacher_hidden, span_table, target_ids, student_logits, proj_weight, norm_gain, head_weight
):
    n_tok = lax.axis_size("tok")
    n_vocab = lax.axis_size("vocab")
    head_full = lax.all_gather(head_weight, "tok", axis=0, tiled=True)
    rows = teacher_hidden.shape[0]
    margin = rows // 4
    extended = padded(teacher_hidden, "tok", margin)
    first_row = lax.axis_index("tok") * rows - margin
    positions = first_row + jnp.arange(rows + 2 * margin, dtype=jnp.int32)
    starts = span_table[:, 0]
    ends = span_table[:, 1]
    member = (
        (positions[None, :] >= starts[:, None]) & (positions[None, :] < ends[:, None])
    ).astype(jnp.bfloat16)
    summed = jnp.dot(member, extended, preferred_element_type=jnp.float32)
    counts = (ends - starts).astype(jnp.float32)
    pooled_part = (summed / counts[:, None]).astype(jnp.bfloat16)
    part = pooled_part.shape[1]
    pooled_blocks = vocab_gather(pooled_part, 0)
    pooled = jnp.swapaxes(pooled_blocks, 0, 1).reshape(rows, n_vocab * part)
    projected_part = lax.dot_general(
        proj_weight, pooled, (((1,), (1,)), ((), ())), preferred_element_type=jnp.float32
    )
    width_part = proj_weight.shape[0]
    width = norm_gain.shape[0]
    projected = vocab_gather(projected_part, 1).reshape(width, rows)
    inverse = lax.rsqrt(jnp.sum(projected * projected, axis=0) / width + EPS)
    normed = (projected * inverse[None, :] * norm_gain[:, None]).astype(jnp.bfloat16)

    student = student_logits.astype(jnp.float32)
    head_logits = lax.dot_general(
        normed, head_full, (((0,), (1,)), ((), ())), preferred_element_type=jnp.float32
    )
    vocab_part = student_logits.shape[1]
    vocab_ids = lax.axis_index("vocab") * vocab_part + jnp.arange(vocab_part, dtype=jnp.int32)
    hit = (vocab_ids[None, :] == target_ids[:, None]).astype(jnp.float32)
    student_top = jnp.max(student, axis=1)
    student_exp = jnp.exp(student - student_top[:, None])
    head_top = jnp.max(head_logits, axis=1)
    head_exp = jnp.exp(head_logits - head_top[:, None])
    stats = jnp.stack(
        [
            student_top,
            jnp.sum(student_exp, axis=1),
            jnp.sum(student_exp * (student - head_logits), axis=1),
            jnp.sum(student_exp * head_logits, axis=1),
            head_top,
            jnp.sum(head_exp, axis=1),
            jnp.sum(head_exp * head_logits, axis=1),
            jnp.sum(hit * head_logits, axis=1),
        ]
    )
    stats = vocab_gather(stats, 2)
    tops = jnp.max(stats, axis=0)
    student_scale = jnp.exp(stats[:, 0] - tops[0])
    head_scale = jnp.exp(stats[:, 4] - tops[4])
    student_total = jnp.sum(stats[:, 1] * student_scale, axis=0)
    student_gap = jnp.sum(stats[:, 2] * student_scale, axis=0) / student_total
    student_head = jnp.sum(stats[:, 3] * student_scale, axis=0) / student_total
    head_total = jnp.sum(stats[:, 5] * head_scale, axis=0)
    head_head = jnp.sum(stats[:, 6] * head_scale, axis=0) / head_total
    picked = jnp.sum(stats[:, 7], axis=0)
    student_lse = tops[0] + jnp.log(student_total)
    head_lse = tops[4] + jnp.log(head_total)
    token_loss = student_gap - student_lse + head_lse + head_lse - picked
    inner = 2.0 * head_head - student_head - picked

    prob_student = jnp.exp(student - student_lse[:, None])
    prob_head = jnp.exp(head_logits - head_lse[:, None])
    logit_grad = (2.0 * prob_head - prob_student - hit).astype(jnp.bfloat16)
    grad_parts = lax.dot_general(
        head_full, logit_grad, (((0,), (1,)), ((), ())), preferred_element_type=jnp.float32
    ).astype(jnp.bfloat16)
    grad_parts, pooled_columns = exchange(
        grad_parts.reshape(n_vocab, width_part, rows), pooled_blocks, 3
    )
    normed_grad = jnp.sum(grad_parts.astype(jnp.float32), axis=0)
    gain_part = lax.dynamic_slice_in_dim(
        norm_gain, lax.axis_index("vocab") * width_part, width_part
    )
    gain_grad = normed_grad * gain_part[:, None]
    scaled_part = projected_part * inverse[None, :]
    out_grad = (inverse[None, :] * (gain_grad - scaled_part * inner[None, :] / width)).astype(
        jnp.bfloat16
    )
    out_grads = tok_gather(out_grad, 4)
    proj_grad = lax.dot_general(
        jnp.swapaxes(out_grads, 0, 1).reshape(width_part, n_tok * rows),
        pooled_columns.reshape(n_tok * rows, -1),
        (((1,), (0,)), ((), ())),
        preferred_element_type=jnp.float32,
    )
    return (token_loss, proj_grad)


def solution(mesh):
    return jax.shard_map(
        on_device,
        mesh=mesh,
        in_specs=(
            P("tok", "vocab"),
            P("tok", None),
            P("tok"),
            P("tok", "vocab"),
            P("vocab", None),
            P(),
            P(("vocab", "tok"), None),
        ),
        out_specs=(P("tok"), P("vocab", "tok")),
        check_vma=False,
    )
```

```python
import functools

import jax
import jax.numpy as jnp
from jax import lax
from jax.experimental import pallas as pl
from jax.experimental.pallas import tpu as pltpu
from jax.sharding import PartitionSpec as P

EPS = 1e-06
MESH = pl.DeviceIdType.MESH


def greet(peers, tok_peers=()):
    barrier = pltpu.get_barrier_semaphore()
    for peer in peers:
        pl.semaphore_signal(barrier, inc=1, device_id={"vocab": peer}, device_id_type=MESH)
    for peer in tok_peers:
        pl.semaphore_signal(barrier, inc=1, device_id={"tok": peer}, device_id_type=MESH)
    pl.semaphore_wait(barrier, len(peers) + len(tok_peers))


def gather_kernel(chips, block, out, send, recv, pass_send, pass_recv, keep):
    me = lax.axis_index("vocab")
    core = lax.rem(me, 2)
    chip = lax.div(me, 2)
    partner = chip * 2 + (1 - core)
    ahead = [lax.rem(chip + step, chips) * 2 + core for step in range(1, chips)]
    behind = [lax.rem(chip + chips - step, chips) * 2 + core for step in range(1, chips)]
    greet(ahead + [partner])
    steps = sorted(range(1, chips), key=lambda step: -min(step, chips - step))
    copies = {}
    for step in steps:
        copies[step] = pltpu.make_async_remote_copy(
            src_ref=block, dst_ref=out.at[me], send_sem=send.at[step], recv_sem=recv.at[step],
            device_id={"vocab": ahead[step - 1]}, device_id_type=MESH,
        )
        copies[step].start()
    own = pltpu.make_async_copy(block, out.at[me], keep)
    own.start()
    passes = [
        pltpu.make_async_remote_copy(
            src_ref=block, dst_ref=out.at[me], send_sem=pass_send.at[0], recv_sem=pass_recv.at[0],
            device_id={"vocab": partner}, device_id_type=MESH,
        )
    ]
    passes[0].start()
    for step in reversed(steps):
        copies[step].wait_recv()
        source = behind[step - 1]
        onward = pltpu.make_async_remote_copy(
            src_ref=out.at[source], dst_ref=out.at[source],
            send_sem=pass_send.at[step], recv_sem=pass_recv.at[step],
            device_id={"vocab": partner}, device_id_type=MESH,
        )
        onward.start()
        passes.append(onward)
    for onward in passes:
        onward.wait()
    for step in steps:
        copies[step].wait_send()
    own.wait()


def vocab_gather(block, collective_id):
    count = lax.axis_size("vocab")
    chips = count // 2
    return pl.pallas_call(
        functools.partial(gather_kernel, chips),
        out_shape=jax.ShapeDtypeStruct((count,) + block.shape, block.dtype),
        in_specs=[pl.BlockSpec(memory_space=pltpu.VMEM)],
        out_specs=pl.BlockSpec(memory_space=pltpu.VMEM),
        scratch_shapes=[pltpu.SemaphoreType.DMA((chips,))] * 4 + [pltpu.SemaphoreType.DMA],
        compiler_params=pltpu.CompilerParams(collective_id=collective_id, has_side_effects=True),
        cost_estimate=pl.CostEstimate(flops=0, bytes_accessed=30_000_000, transcendentals=0),
    )(block)


def exchange_kernel(
    count, n_tok, blocks, pooled, out, columns, send, recv, tok_send, tok_recv, keep
):
    me = lax.axis_index("vocab")
    row = lax.axis_index("tok")
    ahead = [lax.rem(me + step, count) for step in range(1, count)]
    rows_ahead = [lax.rem(row + step, n_tok) for step in range(1, n_tok)]
    part = columns.shape[2]
    each = pooled.shape[2] // part

    def column_block(index):
        start = pl.multiple_of(lax.rem(index, each) * part, part)
        return pooled.at[lax.div(index, each), :, pl.ds(start, part)]

    greet(ahead, rows_ahead)
    copies = [
        pltpu.make_async_copy(blocks.at[me], out.at[me], keep.at[0]),
        pltpu.make_async_copy(column_block(row), columns.at[row], keep.at[1]),
    ]
    for step in sorted(range(1, count), key=lambda step: -min(step, count - step)):
        copies.append(
            pltpu.make_async_remote_copy(
                src_ref=blocks.at[ahead[step - 1]], dst_ref=out.at[me],
                send_sem=send.at[step], recv_sem=recv.at[step],
                device_id={"vocab": ahead[step - 1]}, device_id_type=MESH,
            )
        )
    for step in range(1, n_tok):
        copies.append(
            pltpu.make_async_remote_copy(
                src_ref=column_block(rows_ahead[step - 1]), dst_ref=columns.at[row],
                send_sem=tok_send.at[step], recv_sem=tok_recv.at[step],
                device_id={"tok": rows_ahead[step - 1]}, device_id_type=MESH,
            )
        )
    for copy in copies:
        copy.start()
    for copy in copies:
        copy.wait()


def exchange(blocks, pooled, collective_id):
    count = lax.axis_size("vocab")
    n_tok = lax.axis_size("tok")
    rows = pooled.shape[1]
    part = pooled.shape[0] * pooled.shape[2] // n_tok
    return pl.pallas_call(
        functools.partial(exchange_kernel, count, n_tok),
        out_shape=(
            jax.ShapeDtypeStruct(blocks.shape, blocks.dtype),
            jax.ShapeDtypeStruct((n_tok, rows, part), pooled.dtype),
        ),
        in_specs=[pl.BlockSpec(memory_space=pltpu.VMEM)] * 2,
        out_specs=[pl.BlockSpec(memory_space=pltpu.VMEM)] * 2,
        scratch_shapes=[pltpu.SemaphoreType.DMA((count,))] * 2
        + [pltpu.SemaphoreType.DMA((n_tok,))] * 2
        + [pltpu.SemaphoreType.DMA((2,))],
        compiler_params=pltpu.CompilerParams(collective_id=collective_id, has_side_effects=True),
        cost_estimate=pl.CostEstimate(flops=0, bytes_accessed=30_000_000, transcendentals=0),
    )(blocks, pooled)


SIDE_X = 4


def tok_gather_kernel(
    n_z, split, block, out, x_send, x_recv, z_send, z_recv, xz_send, xz_recv, zx_send, zx_recv, keep
):
    me = lax.axis_index("tok")
    n_x = SIDE_X
    x = lax.rem(me, n_x)
    z = lax.div(me, n_x)
    x_ahead = [z * n_x + lax.rem(x + step, n_x) for step in range(n_x)]
    x_behind = [z * n_x + lax.rem(x + n_x - step, n_x) for step in range(n_x)]
    z_ahead = [lax.rem(z + step, n_z) * n_x + x for step in range(n_z)]
    z_behind = [lax.rem(z + n_z - step, n_z) * n_x + x for step in range(n_z)]
    greet([], x_ahead[1:] + z_ahead[1:])
    first = pl.ds(0, split)
    second = pl.ds(split, block.shape[0] - split)
    far_first = sorted(range(1, n_z), key=lambda step: -min(step, n_z - step))

    def copy(source, index, rows, send, recv, peer):
        made = pltpu.make_async_remote_copy(
            src_ref=source, dst_ref=out.at[index, rows], send_sem=send, recv_sem=recv,
            device_id={"tok": peer}, device_id_type=MESH,
        )
        made.start()
        return made

    own = pltpu.make_async_copy(block, out.at[me], keep)
    own.start()
    along_x = {
        e: copy(block.at[first], me, first, x_send.at[e], x_recv.at[e], x_ahead[e])
        for e in range(1, n_x)
    }
    along_z = {
        d: copy(block.at[second], me, second, z_send.at[d], z_recv.at[d], z_ahead[d])
        for d in far_first
    }
    later = []

    def onward_z(source, index, e):
        for d in far_first:
            slot = e * n_z + d
            later.append(
                copy(source, index, first, xz_send.at[slot], xz_recv.at[slot], z_ahead[d])
            )

    def onward_x(source, index, d):
        for e in (2, 1, 3):
            slot = d * n_x + e
            later.append(
                copy(source, index, second, zx_send.at[slot], zx_recv.at[slot], x_ahead[e])
            )

    onward_x(block.at[second], me, 0)
    onward_z(block.at[first], me, 0)
    arrivals = [("x", 1), ("x", 3), ("z", 1), ("z", 7), ("x", 2), ("z", 2), ("z", 6)]
    arrivals += [("z", 3), ("z", 5), ("z", 4)]
    for axis, step in arrivals:
        if axis == "x":
            along_x[step].wait_recv()
            onward_z(out.at[x_behind[step], first], x_behind[step], step)
        else:
            along_z[step].wait_recv()
            onward_x(out.at[z_behind[step], second], z_behind[step], step)
    for made in later:
        made.wait()
    for made in list(along_x.values()) + list(along_z.values()):
        made.wait_send()
    own.wait()


def tok_gather(block, collective_id):
    n_tok = lax.axis_size("tok")
    n_z = n_tok // SIDE_X
    return pl.pallas_call(
        functools.partial(tok_gather_kernel, n_z, block.shape[0] // 3),
        out_shape=jax.ShapeDtypeStruct((n_tok,) + block.shape, block.dtype),
        in_specs=[pl.BlockSpec(memory_space=pltpu.VMEM)],
        out_specs=pl.BlockSpec(memory_space=pltpu.VMEM),
        scratch_shapes=[pltpu.SemaphoreType.DMA((SIDE_X,))] * 2
        + [pltpu.SemaphoreType.DMA((n_z,))] * 2
        + [pltpu.SemaphoreType.DMA((n_tok,))] * 4
        + [pltpu.SemaphoreType.DMA],
        compiler_params=pltpu.CompilerParams(collective_id=collective_id, has_side_effects=True),
        cost_estimate=pl.CostEstimate(flops=0, bytes_accessed=30_000_000, transcendentals=0),
    )(block)


def cycle_place(cycle, tok, n_z):
    x = lax.rem(tok, SIDE_X)
    z = lax.div(tok, SIDE_X)
    turn = lax.rem(x + z, SIDE_X)
    if cycle == 0:
        return SIDE_X * z + turn
    return SIDE_X * lax.rem(3 * (z + n_z - turn), n_z) + turn


def cycle_device(cycle, place, n_z):
    lap = lax.div(place, SIDE_X)
    turn = lax.rem(place, SIDE_X)
    if cycle == 0:
        return SIDE_X * lap + lax.rem(turn + 2 * n_z - lap, SIDE_X)
    return SIDE_X * lax.rem(3 * lap + turn, n_z) + lax.rem(lap, SIDE_X)


def front_kernel(
    chips, n_tok, teacher, spans, proj_weight, head,
    head_full, pooled, projected,
    extended, ring_send, ring_recv, halo_send, halo_recv,
    y_send, y_recv, core_send, core_recv, keep,
):
    n_z = n_tok // SIDE_X
    laps = n_tok - 1
    tok = lax.axis_index("tok")
    me = lax.axis_index("vocab")
    core = lax.rem(me, 2)
    chip = lax.div(me, 2)
    partner = chip * 2 + (1 - core)
    ahead = [lax.rem(chip + step, chips) * 2 + core for step in range(1, chips)]
    behind = [lax.rem(chip + chips - step, chips) * 2 + core for step in range(1, chips)]
    tok_next = lax.rem(tok + 1, n_tok)
    tok_last = lax.rem(tok + n_tok - 1, n_tok)
    places = [cycle_place(cycle, tok, n_z) for cycle in range(2)]
    targets = []
    for cycle in range(2):
        targets.append(cycle_device(cycle, lax.rem(places[cycle] + 1, n_tok), n_z))
        targets.append(cycle_device(cycle, lax.rem(places[cycle] + n_tok - 1, n_tok), n_z))
    greet(ahead + [partner], targets + [tok_next, tok_last])

    columns = head.shape[1] // 4

    def share(ring):
        return pl.ds(ring * columns, columns)

    def ring_copy(ring, step, source=None):
        back = n_tok - step if ring % 2 == 0 else step
        cycle = ring // 2
        owner = cycle_device(cycle, lax.rem(places[cycle] + back, n_tok), n_z)
        block = head_full.at[owner, :, share(ring)]
        return pltpu.make_async_remote_copy(
            src_ref=block if source is None else source, dst_ref=block,
            send_sem=ring_send.at[ring * laps + step], recv_sem=ring_recv.at[ring * laps + step],
            device_id={"tok": targets[ring]}, device_id_type=MESH,
        )

    def ring_steps(low, high):
        @pl.loop(low, high)
        def _(step):
            for ring in range(4):
                ring_copy(ring, step - 1).wait_recv()
                ring_copy(ring, step).start()

    for ring in range(4):
        ring_copy(ring, 0, head.at[:, share(ring)]).start()
    rows = teacher.shape[0]
    margin = rows // 4
    halos = [
        pltpu.make_async_remote_copy(
            src_ref=teacher.at[pl.ds(rows - margin, margin)], dst_ref=extended.at[pl.ds(0, margin)],
            send_sem=halo_send.at[0], recv_sem=halo_recv.at[0],
            device_id={"tok": tok_next}, device_id_type=MESH,
        ),
        pltpu.make_async_remote_copy(
            src_ref=teacher.at[pl.ds(0, margin)], dst_ref=extended.at[pl.ds(rows + margin, margin)],
            send_sem=halo_send.at[1], recv_sem=halo_recv.at[1],
            device_id={"tok": tok_last}, device_id_type=MESH,
        ),
    ]
    for halo in halos:
        halo.start()
    own = pltpu.make_async_copy(head, head_full.at[tok], keep)
    own.start()
    extended[pl.ds(margin, rows), :] = teacher[...]
    starts = spans[:, 0:1]
    ends = spans[:, 1:2]
    positions = (
        tok * rows - margin + lax.broadcasted_iota(jnp.int32, (rows, rows + 2 * margin), 1)
    )
    member = jnp.where((positions >= starts) & (positions < ends), 1.0, 0.0).astype(jnp.bfloat16)
    counts = (ends - starts).astype(jnp.float32)
    ring_steps(1, 2)
    for halo in halos:
        halo.wait()
    summed = jnp.dot(member, extended[...], preferred_element_type=jnp.float32)
    pooled[me] = (summed / counts).astype(jnp.bfloat16)

    far_first = sorted(range(1, chips), key=lambda step: -min(step, chips - step))

    def vocab_copy(which, out, index, slot, send, recv, peer):
        return pltpu.make_async_remote_copy(
            src_ref=out.at[index], dst_ref=out.at[index],
            send_sem=send.at[which * chips + slot], recv_sem=recv.at[which * chips + slot],
            device_id={"vocab": peer}, device_id_type=MESH,
        )

    def spread(which, out):
        copies = [
            vocab_copy(which, out, me, step, y_send, y_recv, ahead[step - 1]) for step in far_first
        ]
        for copy in copies:
            copy.start()
        own_pass = vocab_copy(which, out, me, 0, core_send, core_recv, partner)
        own_pass.start()
        return copies, [own_pass]

    def pass_on(which, out, copies, passes):
        for copy, step in reversed(list(zip(copies, far_first))):
            copy.wait_recv()
            onward = vocab_copy(which, out, behind[step - 1], step, core_send, core_recv, partner)
            onward.start()
            passes.append(onward)

    copies, passes = spread(0, pooled)
    ring_steps(2, 7)
    pass_on(0, pooled, copies, passes)
    ring_steps(7, 8)
    for onward in passes:
        onward.wait()
    part = pooled.shape[2]
    total = None
    for j in range(2 * chips):
        term = lax.dot_general(
            proj_weight[:, j * part : (j + 1) * part], pooled[j], (((1,), (1,)), ((), ())),
            preferred_element_type=jnp.float32,
        )
        total = term if total is None else total + term
    projected[me] = total
    more, more_passes = spread(1, projected)
    ring_steps(8, 13)
    pass_on(1, projected, more, more_passes)
    ring_steps(13, 14)
    for onward in more_passes:
        onward.wait()
    ring_steps(14, laps)
    for ring in range(4):
        ring_copy(ring, laps - 1).wait_recv()

    @pl.loop(0, laps)
    def _(step):
        for ring in range(4):
            ring_copy(ring, step).wait_send()

    for copy in copies + more:
        copy.wait_send()
    own.wait()


def front(teacher, spans, proj_weight, head, collective_id):
    n_tok = lax.axis_size("tok")
    n_vocab = lax.axis_size("vocab")
    chips = n_vocab // 2
    rows, part = teacher.shape
    sems = [4 * (n_tok - 1)] * 2 + [2] * 2 + [2 * chips] * 4
    return pl.pallas_call(
        functools.partial(front_kernel, chips, n_tok),
        out_shape=(
            jax.ShapeDtypeStruct((n_tok,) + head.shape, head.dtype),
            jax.ShapeDtypeStruct((n_vocab, rows, part), jnp.bfloat16),
            jax.ShapeDtypeStruct((n_vocab, proj_weight.shape[0], rows), jnp.float32),
        ),
        in_specs=[pl.BlockSpec(memory_space=pltpu.VMEM)] * 4,
        out_specs=[pl.BlockSpec(memory_space=pl.ANY)] + [pl.BlockSpec(memory_space=pltpu.VMEM)] * 2,
        scratch_shapes=[pltpu.VMEM((rows + rows // 2, part), jnp.bfloat16)]
        + [pltpu.SemaphoreType.DMA((size,)) for size in sems]
        + [pltpu.SemaphoreType.DMA],
        compiler_params=pltpu.CompilerParams(collective_id=collective_id, has_side_effects=True),
    )(teacher, spans, proj_weight, head)


def on_device(
    teacher_hidden, span_table, target_ids, student_logits, proj_weight, norm_gain, head_weight
):
    n_tok = lax.axis_size("tok")
    n_vocab = lax.axis_size("vocab")
    rows = teacher_hidden.shape[0]
    width_part = proj_weight.shape[0]
    head_full, pooled_blocks, projected = front(
        teacher_hidden, span_table, proj_weight, head_weight, 0
    )
    head_full = head_full.reshape(-1, head_weight.shape[1])
    projected_part = lax.dynamic_index_in_dim(
        projected, lax.axis_index("vocab"), 0, keepdims=False
    )
    width = norm_gain.shape[0]
    projected = projected.reshape(width, rows)
    inverse = lax.rsqrt(jnp.sum(projected * projected, axis=0) / width + EPS)
    normed = (projected * inverse[None, :] * norm_gain[:, None]).astype(jnp.bfloat16)

    student = student_logits.astype(jnp.float32)
    head_logits = lax.dot_general(
        normed, head_full, (((0,), (1,)), ((), ())), preferred_element_type=jnp.float32
    )
    vocab_part = student_logits.shape[1]
    vocab_ids = lax.axis_index("vocab") * vocab_part + jnp.arange(vocab_part, dtype=jnp.int32)
    hit = (vocab_ids[None, :] == target_ids[:, None]).astype(jnp.float32)
    student_top = jnp.max(student, axis=1)
    student_exp = jnp.exp(student - student_top[:, None])
    head_top = jnp.max(head_logits, axis=1)
    head_exp = jnp.exp(head_logits - head_top[:, None])
    stats = jnp.stack(
        [
            student_top,
            jnp.sum(student_exp, axis=1),
            jnp.sum(student_exp * (student - head_logits), axis=1),
            jnp.sum(student_exp * head_logits, axis=1),
            head_top,
            jnp.sum(head_exp, axis=1),
            jnp.sum(head_exp * head_logits, axis=1),
            jnp.sum(hit * head_logits, axis=1),
        ]
    )
    stats = vocab_gather(stats, 2)
    tops = jnp.max(stats, axis=0)
    student_scale = jnp.exp(stats[:, 0] - tops[0])
    head_scale = jnp.exp(stats[:, 4] - tops[4])
    student_total = jnp.sum(stats[:, 1] * student_scale, axis=0)
    student_gap = jnp.sum(stats[:, 2] * student_scale, axis=0) / student_total
    student_head = jnp.sum(stats[:, 3] * student_scale, axis=0) / student_total
    head_total = jnp.sum(stats[:, 5] * head_scale, axis=0)
    head_head = jnp.sum(stats[:, 6] * head_scale, axis=0) / head_total
    picked = jnp.sum(stats[:, 7], axis=0)
    student_lse = tops[0] + jnp.log(student_total)
    head_lse = tops[4] + jnp.log(head_total)
    token_loss = student_gap - student_lse + head_lse + head_lse - picked
    inner = 2.0 * head_head - student_head - picked

    prob_student = jnp.exp(student - student_lse[:, None])
    prob_head = jnp.exp(head_logits - head_lse[:, None])
    logit_grad = (2.0 * prob_head - prob_student - hit).astype(jnp.bfloat16)
    grad_parts = lax.dot_general(
        head_full, logit_grad, (((0,), (1,)), ((), ())), preferred_element_type=jnp.float32
    ).astype(jnp.bfloat16)
    grad_parts, pooled_columns = exchange(
        grad_parts.reshape(n_vocab, width_part, rows), pooled_blocks, 3
    )
    normed_grad = jnp.sum(grad_parts.astype(jnp.float32), axis=0)
    gain_part = lax.dynamic_slice_in_dim(
        norm_gain, lax.axis_index("vocab") * width_part, width_part
    )
    gain_grad = normed_grad * gain_part[:, None]
    scaled_part = projected_part * inverse[None, :]
    out_grad = (inverse[None, :] * (gain_grad - scaled_part * inner[None, :] / width)).astype(
        jnp.bfloat16
    )
    out_grads = tok_gather(out_grad, 4)
    proj_grad = lax.dot_general(
        jnp.swapaxes(out_grads, 0, 1).reshape(width_part, n_tok * rows),
        pooled_columns.reshape(n_tok * rows, -1),
        (((1,), (0,)), ((), ())),
        preferred_element_type=jnp.float32,
    )
    return (token_loss, proj_grad)


def solution(mesh):
    return jax.shard_map(
        on_device,
        mesh=mesh,
        in_specs=(
            P("tok", "vocab"),
            P("tok", None),
            P("tok"),
            P("tok", "vocab"),
            P("vocab", None),
            P(),
            P(("vocab", "tok"), None),
        ),
        out_specs=(P("tok"), P("vocab", "tok")),
        check_vma=False,
    )
```

```python
import functools

import jax
import jax.numpy as jnp
from jax import lax
from jax.experimental import pallas as pl
from jax.experimental.pallas import tpu as pltpu
from jax.sharding import PartitionSpec as P

EPS = 1e-06
MESH = pl.DeviceIdType.MESH


def greet(peers, tok_peers=()):
    barrier = pltpu.get_barrier_semaphore()
    for peer in peers:
        pl.semaphore_signal(barrier, inc=1, device_id={"vocab": peer}, device_id_type=MESH)
    for peer in tok_peers:
        pl.semaphore_signal(barrier, inc=1, device_id={"tok": peer}, device_id_type=MESH)
    pl.semaphore_wait(barrier, len(peers) + len(tok_peers))


def gather_kernel(chips, block, out, send, recv, pass_send, pass_recv, keep):
    me = lax.axis_index("vocab")
    core = lax.rem(me, 2)
    chip = lax.div(me, 2)
    partner = chip * 2 + (1 - core)
    ahead = [lax.rem(chip + step, chips) * 2 + core for step in range(1, chips)]
    behind = [lax.rem(chip + chips - step, chips) * 2 + core for step in range(1, chips)]
    greet(ahead + [partner])
    steps = sorted(range(1, chips), key=lambda step: -min(step, chips - step))
    copies = {}
    for step in steps:
        copies[step] = pltpu.make_async_remote_copy(
            src_ref=block, dst_ref=out.at[me], send_sem=send.at[step], recv_sem=recv.at[step],
            device_id={"vocab": ahead[step - 1]}, device_id_type=MESH,
        )
        copies[step].start()
    own = pltpu.make_async_copy(block, out.at[me], keep)
    own.start()
    passes = [
        pltpu.make_async_remote_copy(
            src_ref=block, dst_ref=out.at[me], send_sem=pass_send.at[0], recv_sem=pass_recv.at[0],
            device_id={"vocab": partner}, device_id_type=MESH,
        )
    ]
    passes[0].start()
    for step in reversed(steps):
        copies[step].wait_recv()
        source = behind[step - 1]
        onward = pltpu.make_async_remote_copy(
            src_ref=out.at[source], dst_ref=out.at[source],
            send_sem=pass_send.at[step], recv_sem=pass_recv.at[step],
            device_id={"vocab": partner}, device_id_type=MESH,
        )
        onward.start()
        passes.append(onward)
    for onward in passes:
        onward.wait()
    for step in steps:
        copies[step].wait_send()
    own.wait()


def vocab_gather(block, collective_id):
    count = lax.axis_size("vocab")
    chips = count // 2
    return pl.pallas_call(
        functools.partial(gather_kernel, chips),
        out_shape=jax.ShapeDtypeStruct((count,) + block.shape, block.dtype),
        in_specs=[pl.BlockSpec(memory_space=pltpu.VMEM)],
        out_specs=pl.BlockSpec(memory_space=pltpu.VMEM),
        scratch_shapes=[pltpu.SemaphoreType.DMA((chips,))] * 4 + [pltpu.SemaphoreType.DMA],
        compiler_params=pltpu.CompilerParams(collective_id=collective_id, has_side_effects=True),
        cost_estimate=pl.CostEstimate(flops=0, bytes_accessed=30_000_000, transcendentals=0),
    )(block)


def exchange_kernel(count, blocks, out, send, recv, keep):
    me = lax.axis_index("vocab")
    ahead = [lax.rem(me + step, count) for step in range(1, count)]
    greet(ahead)
    own = pltpu.make_async_copy(blocks.at[me], out.at[me], keep)
    own.start()
    copies = []
    for step in sorted(range(1, count), key=lambda step: -min(step, count - step)):
        copy = pltpu.make_async_remote_copy(
            src_ref=blocks.at[ahead[step - 1]], dst_ref=out.at[me],
            send_sem=send.at[step], recv_sem=recv.at[step],
            device_id={"vocab": ahead[step - 1]}, device_id_type=MESH,
        )
        copy.start()
        copies.append(copy)
    for copy in copies:
        copy.wait()
    own.wait()


def vocab_exchange(blocks, collective_id):
    count = lax.axis_size("vocab")
    return pl.pallas_call(
        functools.partial(exchange_kernel, count),
        out_shape=jax.ShapeDtypeStruct(blocks.shape, blocks.dtype),
        in_specs=[pl.BlockSpec(memory_space=pltpu.VMEM)],
        out_specs=pl.BlockSpec(memory_space=pltpu.VMEM),
        scratch_shapes=[pltpu.SemaphoreType.DMA((count,))] * 2 + [pltpu.SemaphoreType.DMA],
        compiler_params=pltpu.CompilerParams(collective_id=collective_id, has_side_effects=True),
        cost_estimate=pl.CostEstimate(flops=0, bytes_accessed=30_000_000, transcendentals=0),
    )(blocks)


SIDE_X = 4


def tok_gather_kernel(
    n_z, split, block, out, x_send, x_recv, z_send, z_recv, xz_send, xz_recv, zx_send, zx_recv, keep
):
    me = lax.axis_index("tok")
    n_x = SIDE_X
    x = lax.rem(me, n_x)
    z = lax.div(me, n_x)
    x_ahead = [z * n_x + lax.rem(x + step, n_x) for step in range(n_x)]
    x_behind = [z * n_x + lax.rem(x + n_x - step, n_x) for step in range(n_x)]
    z_ahead = [lax.rem(z + step, n_z) * n_x + x for step in range(n_z)]
    z_behind = [lax.rem(z + n_z - step, n_z) * n_x + x for step in range(n_z)]
    greet([], x_ahead[1:] + z_ahead[1:])
    first = pl.ds(0, split)
    second = pl.ds(split, block.shape[0] - split)
    far_first = sorted(range(1, n_z), key=lambda step: -min(step, n_z - step))

    def copy(source, index, rows, send, recv, peer):
        made = pltpu.make_async_remote_copy(
            src_ref=source, dst_ref=out.at[index, rows], send_sem=send, recv_sem=recv,
            device_id={"tok": peer}, device_id_type=MESH,
        )
        made.start()
        return made

    own = pltpu.make_async_copy(block, out.at[me], keep)
    own.start()
    along_x = {
        e: copy(block.at[first], me, first, x_send.at[e], x_recv.at[e], x_ahead[e])
        for e in range(1, n_x)
    }
    along_z = {
        d: copy(block.at[second], me, second, z_send.at[d], z_recv.at[d], z_ahead[d])
        for d in far_first
    }
    later = []

    def onward_z(source, index, e):
        for d in far_first:
            slot = e * n_z + d
            later.append(
                copy(source, index, first, xz_send.at[slot], xz_recv.at[slot], z_ahead[d])
            )

    def onward_x(source, index, d):
        for e in (2, 1, 3):
            slot = d * n_x + e
            later.append(
                copy(source, index, second, zx_send.at[slot], zx_recv.at[slot], x_ahead[e])
            )

    onward_x(block.at[second], me, 0)
    onward_z(block.at[first], me, 0)
    arrivals = [("x", 1), ("x", 3), ("z", 1), ("z", 7), ("x", 2), ("z", 2), ("z", 6)]
    arrivals += [("z", 3), ("z", 5), ("z", 4)]
    for axis, step in arrivals:
        if axis == "x":
            along_x[step].wait_recv()
            onward_z(out.at[x_behind[step], first], x_behind[step], step)
        else:
            along_z[step].wait_recv()
            onward_x(out.at[z_behind[step], second], z_behind[step], step)
    for made in later:
        made.wait()
    for made in list(along_x.values()) + list(along_z.values()):
        made.wait_send()
    own.wait()


def tok_gather(block, collective_id):
    n_tok = lax.axis_size("tok")
    n_z = n_tok // SIDE_X
    return pl.pallas_call(
        functools.partial(tok_gather_kernel, n_z, block.shape[0] // 3),
        out_shape=jax.ShapeDtypeStruct((n_tok,) + block.shape, block.dtype),
        in_specs=[pl.BlockSpec(memory_space=pltpu.VMEM)],
        out_specs=pl.BlockSpec(memory_space=pltpu.VMEM),
        scratch_shapes=[pltpu.SemaphoreType.DMA((SIDE_X,))] * 2
        + [pltpu.SemaphoreType.DMA((n_z,))] * 2
        + [pltpu.SemaphoreType.DMA((n_tok,))] * 4
        + [pltpu.SemaphoreType.DMA],
        compiler_params=pltpu.CompilerParams(collective_id=collective_id, has_side_effects=True),
        cost_estimate=pl.CostEstimate(flops=0, bytes_accessed=30_000_000, transcendentals=0),
    )(block)


ROW_TILE = 16


def gather_plan(rows, split, n_x, n_z):
    sides = {"x": n_x, "z": n_z}
    free, arriving, plan, whole = {}, [], [], set()

    def send(now, kind, offset, way, hop):
        low, high = gather_rows(rows, split, sides[kind[0]], kind, offset, way, hop)
        link = (kind[0], way)
        free[link] = max(now, free.get(link, 0.0)) + 0.066 * (high - low)
        arriving.append((free[link] + 2.0, len(plan), (kind, offset, way, hop)))
        plan.append((now, "send", (kind, offset, way, hop)))

    for kind in ("xa", "zb", "za", "xb"):
        for way in range(2):
            send(0.0, kind, 0, way, 1)
    while arriving:
        first = min(arriving)
        arriving.remove(first)
        now, _, (kind, offset, way, hop) = first
        plan.append((now, "wait", (kind, offset, way, hop)))
        side = sides[kind[0]]
        if hop < side // 2:
            send(now, kind, offset, way, hop + 1)
        if kind in ("xa", "zb"):
            found = hop if way == 0 else side - hop
            if hop < side // 2 or kind in whole:
                onward = "za" if kind == "xa" else "xb"
                for way_on in range(2):
                    send(now, onward, found, way_on, 1)
            else:
                whole.add(kind)
    return plan


def gather_rows(rows, split, side, kind, offset, way, hop):
    low, high = (0, split) if kind[1] == "a" else (split, rows)
    if hop == side // 2:
        cut = (high - low) // (2 * ROW_TILE) * ROW_TILE
        middle = low + cut if offset % 2 == 0 else high - cut
        return (low, middle) if way == 0 else (middle, high)
    return low, high


def front_kernel(
    chips, n_tok, plan, teacher, spans, proj_weight, head,
    head_full, pooled, projected, column_rows,
    extended, head_send, head_recv, halo_send, halo_recv,
    y_send, y_recv, core_send, core_recv,
    tok_send, tok_recv, row_send, row_recv, keep,
):
    n_x = SIDE_X
    n_z = n_tok // n_x
    tok = lax.axis_index("tok")
    x = lax.rem(tok, n_x)
    z = lax.div(tok, n_x)
    me = lax.axis_index("vocab")
    core = lax.rem(me, 2)
    chip = lax.div(me, 2)
    partner = chip * 2 + (1 - core)
    ahead = [lax.rem(chip + step, chips) * 2 + core for step in range(1, chips)]
    behind = [lax.rem(chip + chips - step, chips) * 2 + core for step in range(1, chips)]
    tok_ahead = [lax.rem(tok + step, n_tok) for step in range(1, n_tok)]
    greet(ahead + [partner], tok_ahead)

    def device(x_back, z_back):
        return lax.rem(z + n_z - z_back, n_z) * n_x + lax.rem(x + n_x - x_back, n_x)

    rows = teacher.shape[0]
    split = rows * 3 // 8 // ROW_TILE * ROW_TILE
    slots = {name: slot for slot, name in enumerate(n for _, act, n in plan if act == "send")}
    started = []

    def head_copy(name, sending):
        kind, offset, way, hop = name
        side = n_x if kind[0] == "x" else n_z
        low, high = gather_rows(rows, split, side, kind, offset, way, hop)
        span = pl.ds(low, high - low)
        along = hop - 1 if sending else hop
        along = along % side if way == 0 else (side - along) % side
        to = side - 1 if way == 0 else 1
        if kind[0] == "x":
            block, peer = device(along, offset), device(to, 0)
        else:
            block, peer = device(offset, along), device(0, to)
        target = head_full.at[block, span]
        own_block = sending and hop == 1 and offset == 0
        return pltpu.make_async_remote_copy(
            src_ref=head.at[span] if own_block else target, dst_ref=target,
            send_sem=head_send.at[slots[name]], recv_sem=head_recv.at[slots[name]],
            device_id={"tok": peer}, device_id_type=MESH,
        )

    margin = rows // 4
    halos = [
        pltpu.make_async_remote_copy(
            src_ref=teacher.at[pl.ds(rows - margin, margin)], dst_ref=extended.at[pl.ds(0, margin)],
            send_sem=halo_send.at[0], recv_sem=halo_recv.at[0],
            device_id={"tok": tok_ahead[0]}, device_id_type=MESH,
        ),
        pltpu.make_async_remote_copy(
            src_ref=teacher.at[pl.ds(0, margin)], dst_ref=extended.at[pl.ds(rows + margin, margin)],
            send_sem=halo_send.at[1], recv_sem=halo_recv.at[1],
            device_id={"tok": tok_ahead[-1]}, device_id_type=MESH,
        ),
    ]
    for halo in halos:
        halo.start()
    own_head = pltpu.make_async_copy(head, head_full.at[tok], keep.at[0])
    own_head.start()
    far_first = sorted(range(1, chips), key=lambda step: -min(step, chips - step))

    def vocab_copy(which, out, index, slot, send, recv, peer):
        return pltpu.make_async_remote_copy(
            src_ref=out.at[index], dst_ref=out.at[index],
            send_sem=send.at[which * chips + slot], recv_sem=recv.at[which * chips + slot],
            device_id={"vocab": peer}, device_id_type=MESH,
        )

    def spread(which, out):
        copies = [
            vocab_copy(which, out, me, step, y_send, y_recv, ahead[step - 1]) for step in far_first
        ]
        for copy in copies:
            copy.start()
        own_pass = vocab_copy(which, out, me, 0, core_send, core_recv, partner)
        own_pass.start()
        return copies, [own_pass]

    def pass_on(which, out, copies, passes):
        for copy, step in reversed(list(zip(copies, far_first))):
            copy.wait_recv()
            onward = vocab_copy(which, out, behind[step - 1], step, core_send, core_recv, partner)
            onward.start()
            passes.append(onward)

    part = pooled.shape[2]
    piece = column_rows.shape[3]
    each = part // piece
    few = column_rows.shape[2]
    kept = {}

    def pool():
        extended[pl.ds(margin, rows), :] = teacher[...]
        starts = spans[:, 0:1]
        ends = spans[:, 1:2]
        positions = (
            tok * rows - margin + lax.broadcasted_iota(jnp.int32, (rows, rows + 2 * margin), 1)
        )
        inside = (positions >= starts) & (positions < ends)
        member = jnp.where(inside, 1.0, 0.0).astype(jnp.bfloat16)
        counts = (ends - starts).astype(jnp.float32)
        for halo in halos:
            halo.wait()
        summed = jnp.dot(member, extended[...], preferred_element_type=jnp.float32)
        pooled[me] = (summed / counts).astype(jnp.bfloat16)
        kept["pooled"] = spread(0, pooled)

    def pass_pooled():
        pass_on(0, pooled, *kept["pooled"])

    def pooled_piece(index):
        start = pl.multiple_of(lax.rem(index, each) * piece, piece)
        first = pl.multiple_of(chip * few, few)
        return pooled.at[lax.div(index, each), pl.ds(first, few), pl.ds(start, piece)]

    def project():
        for onward in kept["pooled"][1]:
            onward.wait()
        total = None
        for j in range(2 * chips):
            term = lax.dot_general(
                proj_weight[:, j * part : (j + 1) * part], pooled[j], (((1,), (1,)), ((), ())),
                preferred_element_type=jnp.float32,
            )
            total = term if total is None else total + term
        projected[me] = total
        kept["projected"] = spread(1, projected)
        pieces = []
        for step in range(1, n_tok):
            pieces.append(
                pltpu.make_async_remote_copy(
                    src_ref=pooled_piece(tok_ahead[step - 1]), dst_ref=column_rows.at[chip, tok],
                    send_sem=tok_send.at[step], recv_sem=tok_recv.at[step],
                    device_id={"tok": tok_ahead[step - 1]}, device_id_type=MESH,
                )
            )
        pieces.append(
            pltpu.make_async_copy(pooled_piece(tok), column_rows.at[chip, tok], keep.at[1])
        )
        for copy in pieces:
            copy.start()
        kept["pieces"] = pieces

    def pass_projected():
        pass_on(1, projected, *kept["projected"])

    def gather_columns():
        for onward in kept["projected"][1]:
            onward.wait()
        for copy in kept["pieces"]:
            copy.wait()
        kept["columns"] = []
        for step in far_first:
            copy = vocab_copy(0, column_rows, chip, step, row_send, row_recv, ahead[step - 1])
            copy.start()
            kept["columns"].append(copy)

    jobs = [
        (4.0, pool), (15.0, pass_pooled), (20.0, project), (33.0, pass_projected),
        (40.0, gather_columns),
    ]
    for now, act, name in plan:
        while jobs and jobs[0][0] <= now:
            jobs.pop(0)[1]()
        copy = head_copy(name, act == "send")
        if act == "send":
            copy.start()
            started.append(copy)
        else:
            copy.wait_recv()
    while jobs:
        jobs.pop(0)[1]()
    for copy in kept["columns"]:
        copy.wait()
    for copy in started + kept["pooled"][0] + kept["projected"][0]:
        copy.wait_send()
    own_head.wait()


def front(teacher, spans, proj_weight, head, collective_id):
    n_tok = lax.axis_size("tok")
    n_vocab = lax.axis_size("vocab")
    chips = n_vocab // 2
    rows, part = teacher.shape
    split = rows * 3 // 8 // ROW_TILE * ROW_TILE
    plan = gather_plan(rows, split, SIDE_X, n_tok // SIDE_X)
    moves = len(plan) // 2
    sems = [moves] * 2 + [2] * 2 + [2 * chips] * 4 + [n_tok] * 2 + [chips] * 2 + [2]
    return pl.pallas_call(
        functools.partial(front_kernel, chips, n_tok, plan),
        out_shape=(
            jax.ShapeDtypeStruct((n_tok,) + head.shape, head.dtype),
            jax.ShapeDtypeStruct((n_vocab, rows, part), jnp.bfloat16),
            jax.ShapeDtypeStruct((n_vocab, proj_weight.shape[0], rows), jnp.float32),
            jax.ShapeDtypeStruct(
                (chips, n_tok, rows // chips, part * n_vocab // n_tok), jnp.bfloat16
            ),
        ),
        in_specs=[pl.BlockSpec(memory_space=pltpu.VMEM)] * 4,
        out_specs=[pl.BlockSpec(memory_space=pl.ANY)] + [pl.BlockSpec(memory_space=pltpu.VMEM)] * 3,
        scratch_shapes=[pltpu.VMEM((rows + rows // 2, part), jnp.bfloat16)]
        + [pltpu.SemaphoreType.DMA((size,)) for size in sems],
        compiler_params=pltpu.CompilerParams(collective_id=collective_id, has_side_effects=True),
    )(teacher, spans, proj_weight, head)


def on_device(
    teacher_hidden, span_table, target_ids, student_logits, proj_weight, norm_gain, head_weight
):
    n_tok = lax.axis_size("tok")
    n_vocab = lax.axis_size("vocab")
    rows = teacher_hidden.shape[0]
    width_part = proj_weight.shape[0]
    head_full, _, projected, column_rows = front(
        teacher_hidden, span_table, proj_weight, head_weight, 0
    )
    head_full = head_full.reshape(-1, head_weight.shape[1])
    projected_part = lax.dynamic_index_in_dim(
        projected, lax.axis_index("vocab"), 0, keepdims=False
    )
    width = norm_gain.shape[0]
    projected = projected.reshape(width, rows)
    inverse = lax.rsqrt(jnp.sum(projected * projected, axis=0) / width + EPS)
    normed = (projected * inverse[None, :] * norm_gain[:, None]).astype(jnp.bfloat16)

    student = student_logits.astype(jnp.float32)
    head_logits = lax.dot_general(
        normed, head_full, (((0,), (1,)), ((), ())), preferred_element_type=jnp.float32
    )
    vocab_part = student_logits.shape[1]
    vocab_ids = lax.axis_index("vocab") * vocab_part + jnp.arange(vocab_part, dtype=jnp.int32)
    hit = (vocab_ids[None, :] == target_ids[:, None]).astype(jnp.float32)
    student_top = jnp.max(student, axis=1)
    student_exp = jnp.exp(student - student_top[:, None])
    head_top = jnp.max(head_logits, axis=1)
    head_exp = jnp.exp(head_logits - head_top[:, None])
    stats = jnp.stack(
        [
            student_top,
            jnp.sum(student_exp, axis=1),
            jnp.sum(student_exp * (student - head_logits), axis=1),
            jnp.sum(student_exp * head_logits, axis=1),
            head_top,
            jnp.sum(head_exp, axis=1),
            jnp.sum(head_exp * head_logits, axis=1),
            jnp.sum(hit * head_logits, axis=1),
        ]
    )
    stats = vocab_gather(stats, 2)
    tops = jnp.max(stats, axis=0)
    student_scale = jnp.exp(stats[:, 0] - tops[0])
    head_scale = jnp.exp(stats[:, 4] - tops[4])
    student_total = jnp.sum(stats[:, 1] * student_scale, axis=0)
    student_gap = jnp.sum(stats[:, 2] * student_scale, axis=0) / student_total
    student_head = jnp.sum(stats[:, 3] * student_scale, axis=0) / student_total
    head_total = jnp.sum(stats[:, 5] * head_scale, axis=0)
    head_head = jnp.sum(stats[:, 6] * head_scale, axis=0) / head_total
    picked = jnp.sum(stats[:, 7], axis=0)
    student_lse = tops[0] + jnp.log(student_total)
    head_lse = tops[4] + jnp.log(head_total)
    token_loss = student_gap - student_lse + head_lse + head_lse - picked
    inner = 2.0 * head_head - student_head - picked

    prob_student = jnp.exp(student - student_lse[:, None])
    prob_head = jnp.exp(head_logits - head_lse[:, None])
    logit_grad = (2.0 * prob_head - prob_student - hit).astype(jnp.bfloat16)
    grad_parts = lax.dot_general(
        head_full, logit_grad, (((0,), (1,)), ((), ())), preferred_element_type=jnp.float32
    ).astype(jnp.bfloat16)
    grad_parts = vocab_exchange(grad_parts.reshape(n_vocab, width_part, rows), 3)
    normed_grad = jnp.sum(grad_parts.astype(jnp.float32), axis=0)
    gain_part = lax.dynamic_slice_in_dim(
        norm_gain, lax.axis_index("vocab") * width_part, width_part
    )
    gain_grad = normed_grad * gain_part[:, None]
    scaled_part = projected_part * inverse[None, :]
    out_grad = (inverse[None, :] * (gain_grad - scaled_part * inner[None, :] / width)).astype(
        jnp.bfloat16
    )
    out_grads = tok_gather(out_grad, 4)
    proj_grad = lax.dot_general(
        jnp.swapaxes(out_grads, 0, 1).reshape(width_part, n_tok * rows),
        jnp.swapaxes(column_rows, 0, 1).reshape(n_tok * rows, -1),
        (((1,), (0,)), ((), ())),
        preferred_element_type=jnp.float32,
    )
    return (token_loss, proj_grad)


def solution(mesh):
    return jax.shard_map(
        on_device,
        mesh=mesh,
        in_specs=(
            P("tok", "vocab"),
            P("tok", None),
            P("tok"),
            P("tok", "vocab"),
            P("vocab", None),
            P(),
            P(("vocab", "tok"), None),
        ),
        out_specs=(P("tok"), P("vocab", "tok")),
        check_vma=False,
    )
```

```python
import functools

import jax
import jax.numpy as jnp
from jax import lax
from jax.experimental import pallas as pl
from jax.experimental.pallas import tpu as pltpu
from jax.sharding import PartitionSpec as P

EPS = 1e-06
MESH = pl.DeviceIdType.MESH


def greet(peers, tok_peers=()):
    barrier = pltpu.get_barrier_semaphore()
    for peer in peers:
        pl.semaphore_signal(barrier, inc=1, device_id={"vocab": peer}, device_id_type=MESH)
    for peer in tok_peers:
        pl.semaphore_signal(barrier, inc=1, device_id={"tok": peer}, device_id_type=MESH)
    pl.semaphore_wait(barrier, len(peers) + len(tok_peers))


def merge_kernel(count, stats, out, held, send, recv, keep):
    me = lax.axis_index("vocab")
    ahead = [lax.rem(me + step, count) for step in range(1, count)]
    greet(ahead)
    copies = [pltpu.make_async_copy(stats, held.at[me], keep)]
    for step in sorted(range(1, count), key=lambda step: -min(step, count - step)):
        copies.append(
            pltpu.make_async_remote_copy(
                src_ref=stats, dst_ref=held.at[me], send_sem=send.at[step], recv_sem=recv.at[step],
                device_id={"vocab": ahead[step - 1]}, device_id_type=MESH,
            )
        )
    for copy in copies:
        copy.start()
    for copy in copies:
        copy.wait()

    def row(index):
        return held[:, index, :]

    def total(values):
        return jnp.sum(values, axis=0, keepdims=True)

    student_top = jnp.max(row(0), axis=0, keepdims=True)
    head_top = jnp.max(row(4), axis=0, keepdims=True)
    student_scale = jnp.exp(row(0) - student_top)
    head_scale = jnp.exp(row(4) - head_top)
    student_total = total(row(1) * student_scale)
    student_gap = total(row(2) * student_scale) / student_total
    student_head = total(row(3) * student_scale) / student_total
    head_total = total(row(5) * head_scale)
    head_head = total(row(6) * head_scale) / head_total
    picked = total(row(7))
    student_lse = student_top + jnp.log(student_total)
    head_lse = head_top + jnp.log(head_total)
    out[0:1, :] = student_lse
    out[1:2, :] = head_lse
    out[2:3, :] = student_gap - student_lse + head_lse + head_lse - picked
    out[3:4, :] = 2.0 * head_head - student_head - picked
    out[4:8, :] = jnp.zeros_like(out[4:8, :])


def vocab_merge(stats, collective_id):
    count = lax.axis_size("vocab")
    return pl.pallas_call(
        functools.partial(merge_kernel, count),
        out_shape=jax.ShapeDtypeStruct(stats.shape, stats.dtype),
        in_specs=[pl.BlockSpec(memory_space=pltpu.VMEM)],
        out_specs=pl.BlockSpec(memory_space=pltpu.VMEM),
        scratch_shapes=[pltpu.VMEM((count,) + stats.shape, stats.dtype)]
        + [pltpu.SemaphoreType.DMA((count,))] * 2
        + [pltpu.SemaphoreType.DMA],
        compiler_params=pltpu.CompilerParams(collective_id=collective_id, has_side_effects=True),
    )(stats)


SIDE_X = 4


def tail_kernel(
    count, n_z, blocks, gain, inverse, shift, out,
    parts, send, recv, x_send, x_recv, z_send, z_recv, on_send, on_recv, keep,
):
    me = lax.axis_index("vocab")
    ahead = [lax.rem(me + step, count) for step in range(1, count)]
    tok = lax.axis_index("tok")
    n_x = SIDE_X
    n_tok = n_x * n_z
    x = lax.rem(tok, n_x)
    z = lax.div(tok, n_x)
    x_ahead = [z * n_x + lax.rem(x + step, n_x) for step in range(n_x)]
    x_behind = [z * n_x + lax.rem(x + n_x - step, n_x) for step in range(n_x)]
    z_ahead = [lax.rem(z + step, n_z) * n_x + x for step in range(n_z)]
    z_behind = [lax.rem(z + n_z - step, n_z) * n_x + x for step in range(n_z)]
    greet(ahead, x_ahead[1:] + z_ahead[1:])
    each = blocks.shape[1] // 3
    pieces = [pl.ds(piece * each, each) for piece in range(3)]
    z_order = sorted(range(1, n_z), key=lambda step: -min(step, n_z - step))
    x_order = sorted(range(1, n_x), key=lambda step: -min(step, n_x - step))
    own = pltpu.make_async_copy(blocks.at[me], parts.at[me], keep)
    own.start()
    exchanged = []
    for piece in range(3):
        copies = []
        for step in sorted(range(1, count), key=lambda step: -min(step, count - step)):
            copies.append(
                pltpu.make_async_remote_copy(
                    src_ref=blocks.at[ahead[step - 1], pieces[piece]],
                    dst_ref=parts.at[me, pieces[piece]],
                    send_sem=send.at[piece * count + step], recv_sem=recv.at[piece * count + step],
                    device_id={"vocab": ahead[step - 1]}, device_id_type=MESH,
                )
            )
            copies[-1].start()
        exchanged.append(copies)
    own.wait()
    first_hops = [{}, {}, {}]
    later = []

    def copy(index, piece, sends, recvs, slot, peer):
        block = out.at[index, pieces[piece]]
        made = pltpu.make_async_remote_copy(
            src_ref=block, dst_ref=block, send_sem=sends.at[slot], recv_sem=recvs.at[slot],
            device_id={"tok": peer}, device_id_type=MESH,
        )
        made.start()
        return made

    def onward(index, piece, far):
        base = piece * n_tok
        if piece == 0:
            for d in z_order:
                later.append(copy(index, piece, on_send, on_recv, base + far * n_z + d, z_ahead[d]))
        else:
            for e in x_order:
                later.append(copy(index, piece, on_send, on_recv, base + far * n_x + e, x_ahead[e]))

    def reduce_piece(piece):
        for made in exchanged[piece]:
            made.wait_recv()
        rows = slice(piece * each, (piece + 1) * each)
        total = parts[0, rows, :].astype(jnp.float32)
        for index in range(1, count):
            total = total + parts[index, rows, :].astype(jnp.float32)
        grad = inverse[...] * (total * gain[rows, :] - shift[rows, :])
        out[tok, rows, :] = grad.astype(out.dtype)
        if piece == 0:
            for e in x_order:
                first_hops[piece][e] = copy(tok, piece, x_send, x_recv, e, x_ahead[e])
        else:
            for d in z_order:
                slot = piece * n_z + d
                first_hops[piece][d] = copy(tok, piece, z_send, z_recv, slot, z_ahead[d])
        onward(tok, piece, 0)

    def pass_on(piece):
        behind = x_behind if piece == 0 else z_behind
        for step in reversed(x_order if piece == 0 else z_order):
            first_hops[piece][step].wait_recv()
            onward(behind[step], piece, step)

    reduce_piece(0)
    reduce_piece(1)
    pass_on(0)
    reduce_piece(2)
    pass_on(1)
    pass_on(2)
    for made in later:
        made.wait()
    for piece in range(3):
        for made in list(first_hops[piece].values()) + exchanged[piece]:
            made.wait_send()


def tail(blocks, gain, inverse, shift, collective_id):
    count = lax.axis_size("vocab")
    n_tok = lax.axis_size("tok")
    n_z = n_tok // SIDE_X
    sems = [3 * count] * 2 + [SIDE_X] * 2 + [3 * n_z] * 2 + [3 * n_tok] * 2
    return pl.pallas_call(
        functools.partial(tail_kernel, count, n_z),
        out_shape=jax.ShapeDtypeStruct((n_tok,) + blocks.shape[1:], blocks.dtype),
        in_specs=[pl.BlockSpec(memory_space=pltpu.VMEM)] * 4,
        out_specs=pl.BlockSpec(memory_space=pltpu.VMEM),
        scratch_shapes=[pltpu.VMEM(blocks.shape, blocks.dtype)]
        + [pltpu.SemaphoreType.DMA((size,)) for size in sems]
        + [pltpu.SemaphoreType.DMA],
        compiler_params=pltpu.CompilerParams(collective_id=collective_id, has_side_effects=True),
    )(blocks, gain, inverse, shift)


ROW_TILE = 16


def gather_plan(rows, split, n_x, n_z):
    sides = {"x": n_x, "z": n_z}
    free, arriving, plan, whole = {}, [], [], set()

    def send(now, kind, offset, way, hop):
        low, high = gather_rows(rows, split, sides[kind[0]], kind, offset, way, hop)
        link = (kind[0], way)
        free[link] = max(now, free.get(link, 0.0)) + 0.066 * (high - low)
        arriving.append((free[link] + 2.0, len(plan), (kind, offset, way, hop)))
        plan.append((now, "send", (kind, offset, way, hop)))

    for kind in ("xa", "zb", "za", "xb"):
        for way in range(2):
            send(0.0, kind, 0, way, 1)
    while arriving:
        first = min(arriving)
        arriving.remove(first)
        now, _, (kind, offset, way, hop) = first
        plan.append((now, "wait", (kind, offset, way, hop)))
        side = sides[kind[0]]
        if hop < side // 2:
            send(now, kind, offset, way, hop + 1)
        if kind in ("xa", "zb"):
            found = hop if way == 0 else side - hop
            if hop < side // 2 or kind in whole:
                onward = "za" if kind == "xa" else "xb"
                for way_on in range(2):
                    send(now, onward, found, way_on, 1)
            else:
                whole.add(kind)
    return plan


def gather_rows(rows, split, side, kind, offset, way, hop):
    low, high = (0, split) if kind[1] == "a" else (split, rows)
    if hop == side // 2:
        cut = (high - low) // (2 * ROW_TILE) * ROW_TILE
        middle = low + cut if offset % 2 == 0 else high - cut
        return (low, middle) if way == 0 else (middle, high)
    return low, high


def front_kernel(
    chips, n_tok, plan, teacher, spans, proj_weight, head,
    head_full, pooled, projected, column_rows,
    extended, head_send, head_recv, halo_send, halo_recv,
    y_send, y_recv, core_send, core_recv,
    tok_send, tok_recv, row_send, row_recv, keep,
):
    n_x = SIDE_X
    n_z = n_tok // n_x
    tok = lax.axis_index("tok")
    x = lax.rem(tok, n_x)
    z = lax.div(tok, n_x)
    me = lax.axis_index("vocab")
    core = lax.rem(me, 2)
    chip = lax.div(me, 2)
    partner = chip * 2 + (1 - core)
    ahead = [lax.rem(chip + step, chips) * 2 + core for step in range(1, chips)]
    behind = [lax.rem(chip + chips - step, chips) * 2 + core for step in range(1, chips)]
    tok_ahead = [lax.rem(tok + step, n_tok) for step in range(1, n_tok)]
    greet(ahead + [partner], tok_ahead)

    def device(x_back, z_back):
        return lax.rem(z + n_z - z_back, n_z) * n_x + lax.rem(x + n_x - x_back, n_x)

    rows = teacher.shape[0]
    split = rows * 3 // 8 // ROW_TILE * ROW_TILE
    slots = {name: slot for slot, name in enumerate(n for _, act, n in plan if act == "send")}
    started = []

    def head_copy(name, sending):
        kind, offset, way, hop = name
        side = n_x if kind[0] == "x" else n_z
        low, high = gather_rows(rows, split, side, kind, offset, way, hop)
        span = pl.ds(low, high - low)
        along = hop - 1 if sending else hop
        along = along % side if way == 0 else (side - along) % side
        to = side - 1 if way == 0 else 1
        if kind[0] == "x":
            block, peer = device(along, offset), device(to, 0)
        else:
            block, peer = device(offset, along), device(0, to)
        target = head_full.at[block, span]
        own_block = sending and hop == 1 and offset == 0
        return pltpu.make_async_remote_copy(
            src_ref=head.at[span] if own_block else target, dst_ref=target,
            send_sem=head_send.at[slots[name]], recv_sem=head_recv.at[slots[name]],
            device_id={"tok": peer}, device_id_type=MESH,
        )

    margin = rows // 4
    halos = [
        pltpu.make_async_remote_copy(
            src_ref=teacher.at[pl.ds(rows - margin, margin)], dst_ref=extended.at[pl.ds(0, margin)],
            send_sem=halo_send.at[0], recv_sem=halo_recv.at[0],
            device_id={"tok": tok_ahead[0]}, device_id_type=MESH,
        ),
        pltpu.make_async_remote_copy(
            src_ref=teacher.at[pl.ds(0, margin)], dst_ref=extended.at[pl.ds(rows + margin, margin)],
            send_sem=halo_send.at[1], recv_sem=halo_recv.at[1],
            device_id={"tok": tok_ahead[-1]}, device_id_type=MESH,
        ),
    ]
    for halo in halos:
        halo.start()
    own_head = pltpu.make_async_copy(head, head_full.at[tok], keep.at[0])
    own_head.start()
    far_first = sorted(range(1, chips), key=lambda step: -min(step, chips - step))

    def vocab_copy(which, out, index, slot, send, recv, peer):
        return pltpu.make_async_remote_copy(
            src_ref=out.at[index], dst_ref=out.at[index],
            send_sem=send.at[which * chips + slot], recv_sem=recv.at[which * chips + slot],
            device_id={"vocab": peer}, device_id_type=MESH,
        )

    def spread(which, out):
        copies = [
            vocab_copy(which, out, me, step, y_send, y_recv, ahead[step - 1]) for step in far_first
        ]
        for copy in copies:
            copy.start()
        own_pass = vocab_copy(which, out, me, 0, core_send, core_recv, partner)
        own_pass.start()
        return copies, [own_pass]

    def pass_on(which, out, copies, passes):
        for copy, step in reversed(list(zip(copies, far_first))):
            copy.wait_recv()
            onward = vocab_copy(which, out, behind[step - 1], step, core_send, core_recv, partner)
            onward.start()
            passes.append(onward)

    part = pooled.shape[2]
    piece = column_rows.shape[3]
    each = part // piece
    few = column_rows.shape[2]
    kept = {}

    def pool():
        extended[pl.ds(margin, rows), :] = teacher[...]
        starts = spans[:, 0:1]
        ends = spans[:, 1:2]
        positions = (
            tok * rows - margin + lax.broadcasted_iota(jnp.int32, (rows, rows + 2 * margin), 1)
        )
        inside = (positions >= starts) & (positions < ends)
        member = jnp.where(inside, 1.0, 0.0).astype(jnp.bfloat16)
        counts = (ends - starts).astype(jnp.float32)
        for halo in halos:
            halo.wait()
        summed = jnp.dot(member, extended[...], preferred_element_type=jnp.float32)
        pooled[me] = (summed / counts).astype(jnp.bfloat16)
        kept["pooled"] = spread(0, pooled)

    def pass_pooled():
        pass_on(0, pooled, *kept["pooled"])

    def pooled_piece(index):
        start = pl.multiple_of(lax.rem(index, each) * piece, piece)
        first = pl.multiple_of(chip * few, few)
        return pooled.at[lax.div(index, each), pl.ds(first, few), pl.ds(start, piece)]

    def project():
        for onward in kept["pooled"][1]:
            onward.wait()
        total = None
        for j in range(2 * chips):
            term = lax.dot_general(
                proj_weight[:, j * part : (j + 1) * part], pooled[j], (((1,), (1,)), ((), ())),
                preferred_element_type=jnp.float32,
            )
            total = term if total is None else total + term
        projected[me] = total
        kept["projected"] = spread(1, projected)
        pieces = []
        for step in range(1, n_tok):
            pieces.append(
                pltpu.make_async_remote_copy(
                    src_ref=pooled_piece(tok_ahead[step - 1]), dst_ref=column_rows.at[chip, tok],
                    send_sem=tok_send.at[step], recv_sem=tok_recv.at[step],
                    device_id={"tok": tok_ahead[step - 1]}, device_id_type=MESH,
                )
            )
        pieces.append(
            pltpu.make_async_copy(pooled_piece(tok), column_rows.at[chip, tok], keep.at[1])
        )
        for copy in pieces:
            copy.start()
        kept["pieces"] = pieces

    def pass_projected():
        pass_on(1, projected, *kept["projected"])

    def gather_columns():
        for onward in kept["projected"][1]:
            onward.wait()
        for copy in kept["pieces"]:
            copy.wait()
        kept["columns"] = []
        for step in far_first:
            copy = vocab_copy(0, column_rows, chip, step, row_send, row_recv, ahead[step - 1])
            copy.start()
            kept["columns"].append(copy)

    jobs = [
        (4.0, pool), (15.0, pass_pooled), (20.0, project), (33.0, pass_projected),
        (40.0, gather_columns),
    ]
    for now, act, name in plan:
        while jobs and jobs[0][0] <= now:
            jobs.pop(0)[1]()
        copy = head_copy(name, act == "send")
        if act == "send":
            copy.start()
            started.append(copy)
        else:
            copy.wait_recv()
    while jobs:
        jobs.pop(0)[1]()
    for copy in kept["columns"]:
        copy.wait()
    for copy in started + kept["pooled"][0] + kept["projected"][0]:
        copy.wait_send()
    own_head.wait()


def front(teacher, spans, proj_weight, head, collective_id):
    n_tok = lax.axis_size("tok")
    n_vocab = lax.axis_size("vocab")
    chips = n_vocab // 2
    rows, part = teacher.shape
    split = rows * 3 // 8 // ROW_TILE * ROW_TILE
    plan = gather_plan(rows, split, SIDE_X, n_tok // SIDE_X)
    moves = len(plan) // 2
    sems = [moves] * 2 + [2] * 2 + [2 * chips] * 4 + [n_tok] * 2 + [chips] * 2 + [2]
    return pl.pallas_call(
        functools.partial(front_kernel, chips, n_tok, plan),
        out_shape=(
            jax.ShapeDtypeStruct((n_tok,) + head.shape, head.dtype),
            jax.ShapeDtypeStruct((n_vocab, rows, part), jnp.bfloat16),
            jax.ShapeDtypeStruct((n_vocab, proj_weight.shape[0], rows), jnp.float32),
            jax.ShapeDtypeStruct(
                (chips, n_tok, rows // chips, part * n_vocab // n_tok), jnp.bfloat16
            ),
        ),
        in_specs=[pl.BlockSpec(memory_space=pltpu.VMEM)] * 4,
        out_specs=[pl.BlockSpec(memory_space=pl.ANY)] + [pl.BlockSpec(memory_space=pltpu.VMEM)] * 3,
        scratch_shapes=[pltpu.VMEM((rows + rows // 2, part), jnp.bfloat16)]
        + [pltpu.SemaphoreType.DMA((size,)) for size in sems],
        compiler_params=pltpu.CompilerParams(collective_id=collective_id, has_side_effects=True),
    )(teacher, spans, proj_weight, head)


def on_device(
    teacher_hidden, span_table, target_ids, student_logits, proj_weight, norm_gain, head_weight
):
    n_tok = lax.axis_size("tok")
    n_vocab = lax.axis_size("vocab")
    rows = teacher_hidden.shape[0]
    width_part = proj_weight.shape[0]
    head_full, _, projected, column_rows = front(
        teacher_hidden, span_table, proj_weight, head_weight, 0
    )
    head_full = head_full.reshape(-1, head_weight.shape[1])
    projected_part = lax.dynamic_index_in_dim(
        projected, lax.axis_index("vocab"), 0, keepdims=False
    )
    width = norm_gain.shape[0]
    projected = projected.reshape(width, rows)
    inverse = lax.rsqrt(jnp.sum(projected * projected, axis=0) / width + EPS)
    normed = (projected * inverse[None, :] * norm_gain[:, None]).astype(jnp.bfloat16)

    student = student_logits.astype(jnp.float32)
    head_logits = lax.dot_general(
        normed, head_full, (((0,), (1,)), ((), ())), preferred_element_type=jnp.float32
    )
    vocab_part = student_logits.shape[1]
    vocab_ids = lax.axis_index("vocab") * vocab_part + jnp.arange(vocab_part, dtype=jnp.int32)
    hit = (vocab_ids[None, :] == target_ids[:, None]).astype(jnp.float32)
    student_top = jnp.max(student, axis=1)
    student_exp = jnp.exp(student - student_top[:, None])
    head_top = jnp.max(head_logits, axis=1)
    head_exp = jnp.exp(head_logits - head_top[:, None])
    stats = jnp.stack(
        [
            student_top,
            jnp.sum(student_exp, axis=1),
            jnp.sum(student_exp * (student - head_logits), axis=1),
            jnp.sum(student_exp * head_logits, axis=1),
            head_top,
            jnp.sum(head_exp, axis=1),
            jnp.sum(head_exp * head_logits, axis=1),
            jnp.sum(hit * head_logits, axis=1),
        ]
    )
    merged = vocab_merge(stats, 1)
    student_lse, head_lse, token_loss, inner = (merged[index] for index in range(4))

    prob_student = jnp.exp(student - student_lse[:, None])
    prob_head = jnp.exp(head_logits - head_lse[:, None])
    logit_grad = (2.0 * prob_head - prob_student - hit).astype(jnp.bfloat16)
    grad_parts = lax.dot_general(
        head_full, logit_grad, (((0,), (1,)), ((), ())), preferred_element_type=jnp.float32
    ).astype(jnp.bfloat16)
    gain_part = lax.dynamic_slice_in_dim(
        norm_gain, lax.axis_index("vocab") * width_part, width_part
    )
    scaled_part = projected_part * inverse[None, :]
    out_grads = tail(
        grad_parts.reshape(n_vocab, width_part, rows),
        gain_part[:, None],
        inverse[None, :],
        scaled_part * inner[None, :] / width,
        2,
    )
    proj_grad = lax.dot_general(
        jnp.swapaxes(out_grads, 0, 1).reshape(width_part, n_tok * rows),
        jnp.swapaxes(column_rows, 0, 1).reshape(n_tok * rows, -1),
        (((1,), (0,)), ((), ())),
        preferred_element_type=jnp.float32,
    )
    return (token_loss, proj_grad)


def solution(mesh):
    return jax.shard_map(
        on_device,
        mesh=mesh,
        in_specs=(
            P("tok", "vocab"),
            P("tok", None),
            P("tok"),
            P("tok", "vocab"),
            P("vocab", None),
            P(),
            P(("vocab", "tok"), None),
        ),
        out_specs=(P("tok"), P("vocab", "tok")),
        check_vma=False,
    )
```

```python
import functools

import jax
import jax.numpy as jnp
from jax import lax
from jax.experimental import pallas as pl
from jax.experimental.pallas import tpu as pltpu
from jax.sharding import PartitionSpec as P

EPS = 1e-06
MESH = pl.DeviceIdType.MESH


def greet(peers, tok_peers=()):
    barrier = pltpu.get_barrier_semaphore()
    for peer in peers:
        pl.semaphore_signal(barrier, inc=1, device_id={"vocab": peer}, device_id_type=MESH)
    for peer in tok_peers:
        pl.semaphore_signal(barrier, inc=1, device_id={"tok": peer}, device_id_type=MESH)
    pl.semaphore_wait(barrier, len(peers) + len(tok_peers))


def merge_kernel(count, stats, out, held, send, recv, keep):
    me = lax.axis_index("vocab")
    ahead = [lax.rem(me + step, count) for step in range(1, count)]
    greet(ahead)
    copies = [pltpu.make_async_copy(stats, held.at[me], keep)]
    for step in sorted(range(1, count), key=lambda step: -min(step, count - step)):
        copies.append(
            pltpu.make_async_remote_copy(
                src_ref=stats, dst_ref=held.at[me], send_sem=send.at[step], recv_sem=recv.at[step],
                device_id={"vocab": ahead[step - 1]}, device_id_type=MESH,
            )
        )
    for copy in copies:
        copy.start()
    for copy in copies:
        copy.wait()

    def row(index):
        return held[:, index, :]

    def total(values):
        return jnp.sum(values, axis=0, keepdims=True)

    student_top = jnp.max(row(0), axis=0, keepdims=True)
    head_top = jnp.max(row(4), axis=0, keepdims=True)
    student_scale = jnp.exp(row(0) - student_top)
    head_scale = jnp.exp(row(4) - head_top)
    student_total = total(row(1) * student_scale)
    student_gap = total(row(2) * student_scale) / student_total
    student_head = total(row(3) * student_scale) / student_total
    head_total = total(row(5) * head_scale)
    head_head = total(row(6) * head_scale) / head_total
    picked = total(row(7))
    student_lse = student_top + jnp.log(student_total)
    head_lse = head_top + jnp.log(head_total)
    out[0:1, :] = student_lse
    out[1:2, :] = head_lse
    out[2:3, :] = student_gap - student_lse + head_lse + head_lse - picked
    out[3:4, :] = 2.0 * head_head - student_head - picked
    out[4:8, :] = jnp.zeros_like(out[4:8, :])


def vocab_merge(stats, collective_id):
    count = lax.axis_size("vocab")
    return pl.pallas_call(
        functools.partial(merge_kernel, count),
        out_shape=jax.ShapeDtypeStruct(stats.shape, stats.dtype),
        in_specs=[pl.BlockSpec(memory_space=pltpu.VMEM)],
        out_specs=pl.BlockSpec(memory_space=pltpu.VMEM),
        scratch_shapes=[pltpu.VMEM((count,) + stats.shape, stats.dtype)]
        + [pltpu.SemaphoreType.DMA((count,))] * 2
        + [pltpu.SemaphoreType.DMA],
        compiler_params=pltpu.CompilerParams(collective_id=collective_id, has_side_effects=True),
    )(stats)


SIDE_X = 4


def tail_kernel(
    count, n_z, blocks, gain, inverse, shift, out,
    parts, send, recv, x_send, x_recv, z_send, z_recv, on_send, on_recv, keep,
):
    me = lax.axis_index("vocab")
    ahead = [lax.rem(me + step, count) for step in range(1, count)]
    tok = lax.axis_index("tok")
    n_x = SIDE_X
    n_tok = n_x * n_z
    x = lax.rem(tok, n_x)
    z = lax.div(tok, n_x)
    x_ahead = [z * n_x + lax.rem(x + step, n_x) for step in range(n_x)]
    x_behind = [z * n_x + lax.rem(x + n_x - step, n_x) for step in range(n_x)]
    z_ahead = [lax.rem(z + step, n_z) * n_x + x for step in range(n_z)]
    z_behind = [lax.rem(z + n_z - step, n_z) * n_x + x for step in range(n_z)]
    greet(ahead, x_ahead[1:] + z_ahead[1:])
    each = blocks.shape[1] // 3
    pieces = [pl.ds(piece * each, each) for piece in range(3)]
    z_order = sorted(range(1, n_z), key=lambda step: -min(step, n_z - step))
    x_order = sorted(range(1, n_x), key=lambda step: -min(step, n_x - step))
    own = pltpu.make_async_copy(blocks.at[me], parts.at[me], keep)
    own.start()
    exchanged = []
    for piece in range(3):
        copies = []
        for step in sorted(range(1, count), key=lambda step: -min(step, count - step)):
            copies.append(
                pltpu.make_async_remote_copy(
                    src_ref=blocks.at[ahead[step - 1], pieces[piece]],
                    dst_ref=parts.at[me, pieces[piece]],
                    send_sem=send.at[piece * count + step], recv_sem=recv.at[piece * count + step],
                    device_id={"vocab": ahead[step - 1]}, device_id_type=MESH,
                )
            )
            copies[-1].start()
        exchanged.append(copies)
    own.wait()
    first_hops = [{}, {}, {}]
    later = []

    def copy(index, piece, sends, recvs, slot, peer):
        block = out.at[index, pieces[piece]]
        made = pltpu.make_async_remote_copy(
            src_ref=block, dst_ref=block, send_sem=sends.at[slot], recv_sem=recvs.at[slot],
            device_id={"tok": peer}, device_id_type=MESH,
        )
        made.start()
        return made

    def onward(index, piece, far):
        base = piece * n_tok
        if piece == 0:
            for d in z_order:
                later.append(copy(index, piece, on_send, on_recv, base + far * n_z + d, z_ahead[d]))
        else:
            for e in x_order:
                later.append(copy(index, piece, on_send, on_recv, base + far * n_x + e, x_ahead[e]))

    def reduce_piece(piece):
        for made in exchanged[piece]:
            made.wait_recv()
        rows = slice(piece * each, (piece + 1) * each)
        total = parts[0, rows, :].astype(jnp.float32)
        for index in range(1, count):
            total = total + parts[index, rows, :].astype(jnp.float32)
        grad = inverse[...] * (total * gain[rows, :] - shift[rows, :])
        out[tok, rows, :] = grad.astype(out.dtype)
        if piece == 0:
            for e in x_order:
                first_hops[piece][e] = copy(tok, piece, x_send, x_recv, e, x_ahead[e])
        else:
            for d in z_order:
                slot = piece * n_z + d
                first_hops[piece][d] = copy(tok, piece, z_send, z_recv, slot, z_ahead[d])
        onward(tok, piece, 0)

    def pass_on(piece):
        behind = x_behind if piece == 0 else z_behind
        for step in reversed(x_order if piece == 0 else z_order):
            first_hops[piece][step].wait_recv()
            onward(behind[step], piece, step)

    reduce_piece(0)
    reduce_piece(1)
    pass_on(0)
    reduce_piece(2)
    pass_on(1)
    pass_on(2)
    for made in later:
        made.wait()
    for piece in range(3):
        for made in list(first_hops[piece].values()) + exchanged[piece]:
            made.wait_send()


def tail(blocks, gain, inverse, shift, collective_id):
    count = lax.axis_size("vocab")
    n_tok = lax.axis_size("tok")
    n_z = n_tok // SIDE_X
    sems = [3 * count] * 2 + [SIDE_X] * 2 + [3 * n_z] * 2 + [3 * n_tok] * 2
    return pl.pallas_call(
        functools.partial(tail_kernel, count, n_z),
        out_shape=jax.ShapeDtypeStruct((n_tok,) + blocks.shape[1:], blocks.dtype),
        in_specs=[pl.BlockSpec(memory_space=pltpu.VMEM)] * 4,
        out_specs=pl.BlockSpec(memory_space=pltpu.VMEM),
        scratch_shapes=[pltpu.VMEM(blocks.shape, blocks.dtype)]
        + [pltpu.SemaphoreType.DMA((size,)) for size in sems]
        + [pltpu.SemaphoreType.DMA],
        compiler_params=pltpu.CompilerParams(collective_id=collective_id, has_side_effects=True),
    )(blocks, gain, inverse, shift)


ROW_TILE = 16


def gather_plan(rows, split, n_x, n_z):
    sides = {"x": n_x, "z": n_z}
    free, arriving, plan, whole = {}, [], [], set()

    def send(now, kind, offset, way, hop):
        low, high = gather_rows(rows, split, sides[kind[0]], kind, offset, way, hop)
        link = (kind[0], way)
        free[link] = max(now, free.get(link, 0.0)) + 0.066 * (high - low)
        arriving.append((free[link] + 2.0, len(plan), (kind, offset, way, hop)))
        plan.append((now, "send", (kind, offset, way, hop)))

    for kind in ("xa", "zb", "za", "xb"):
        for way in range(2):
            send(0.0, kind, 0, way, 1)
    while arriving:
        first = min(arriving)
        arriving.remove(first)
        now, _, (kind, offset, way, hop) = first
        plan.append((now, "wait", (kind, offset, way, hop)))
        side = sides[kind[0]]
        if hop < side // 2:
            send(now, kind, offset, way, hop + 1)
        if kind in ("xa", "zb"):
            found = hop if way == 0 else side - hop
            if hop < side // 2 or kind in whole:
                onward = "za" if kind == "xa" else "xb"
                for way_on in range(2):
                    send(now, onward, found, way_on, 1)
            else:
                whole.add(kind)
    return plan


def gather_rows(rows, split, side, kind, offset, way, hop):
    low, high = (0, split) if kind[1] == "a" else (split, rows)
    if hop == side // 2:
        cut = (high - low) // (2 * ROW_TILE) * ROW_TILE
        middle = low + cut if offset % 2 == 0 else high - cut
        return (low, middle) if way == 0 else (middle, high)
    return low, high


def front_kernel(
    chips, n_tok, plan, teacher, spans, proj_weight, head,
    head_full, pooled, projected, column_rows,
    extended, head_send, head_recv, halo_send, halo_recv,
    y_send, y_recv, core_send, core_recv,
    tok_send, tok_recv, row_send, row_recv, keep,
):
    n_x = SIDE_X
    n_z = n_tok // n_x
    tok = lax.axis_index("tok")
    x = lax.rem(tok, n_x)
    z = lax.div(tok, n_x)
    me = lax.axis_index("vocab")
    core = lax.rem(me, 2)
    chip = lax.div(me, 2)
    partner = chip * 2 + (1 - core)
    ahead = [lax.rem(chip + step, chips) * 2 + core for step in range(1, chips)]
    behind = [lax.rem(chip + chips - step, chips) * 2 + core for step in range(1, chips)]
    tok_ahead = [lax.rem(tok + step, n_tok) for step in range(1, n_tok)]
    greet(ahead + [partner], tok_ahead)

    def device(x_back, z_back):
        return lax.rem(z + n_z - z_back, n_z) * n_x + lax.rem(x + n_x - x_back, n_x)

    rows = teacher.shape[0]
    split = rows * 3 // 8 // ROW_TILE * ROW_TILE
    slots = {name: slot for slot, name in enumerate(n for _, act, n in plan if act == "send")}
    started = []

    def head_copy(name, sending):
        kind, offset, way, hop = name
        side = n_x if kind[0] == "x" else n_z
        low, high = gather_rows(rows, split, side, kind, offset, way, hop)
        span = pl.ds(low, high - low)
        along = hop - 1 if sending else hop
        along = along % side if way == 0 else (side - along) % side
        to = side - 1 if way == 0 else 1
        if kind[0] == "x":
            block, peer = device(along, offset), device(to, 0)
        else:
            block, peer = device(offset, along), device(0, to)
        target = head_full.at[block, span]
        own_block = sending and hop == 1 and offset == 0
        return pltpu.make_async_remote_copy(
            src_ref=head.at[span] if own_block else target, dst_ref=target,
            send_sem=head_send.at[slots[name]], recv_sem=head_recv.at[slots[name]],
            device_id={"tok": peer}, device_id_type=MESH,
        )

    margin = rows // 4
    halos = [
        pltpu.make_async_remote_copy(
            src_ref=teacher.at[pl.ds(rows - margin, margin)], dst_ref=extended.at[pl.ds(0, margin)],
            send_sem=halo_send.at[0], recv_sem=halo_recv.at[0],
            device_id={"tok": tok_ahead[0]}, device_id_type=MESH,
        ),
        pltpu.make_async_remote_copy(
            src_ref=teacher.at[pl.ds(0, margin)], dst_ref=extended.at[pl.ds(rows + margin, margin)],
            send_sem=halo_send.at[1], recv_sem=halo_recv.at[1],
            device_id={"tok": tok_ahead[-1]}, device_id_type=MESH,
        ),
    ]
    for halo in halos:
        halo.start()
    own_head = pltpu.make_async_copy(head, head_full.at[tok], keep.at[0])
    own_head.start()
    far_first = sorted(range(1, chips), key=lambda step: -min(step, chips - step))

    def vocab_copy(which, out, index, slot, send, recv, peer):
        return pltpu.make_async_remote_copy(
            src_ref=out.at[index], dst_ref=out.at[index],
            send_sem=send.at[which * chips + slot], recv_sem=recv.at[which * chips + slot],
            device_id={"vocab": peer}, device_id_type=MESH,
        )

    def spread(which, out):
        copies = [
            vocab_copy(which, out, me, step, y_send, y_recv, ahead[step - 1]) for step in far_first
        ]
        for copy in copies:
            copy.start()
        own_pass = vocab_copy(which, out, me, 0, core_send, core_recv, partner)
        own_pass.start()
        return copies, [own_pass]

    def pass_on(which, out, copies, passes):
        for copy, step in reversed(list(zip(copies, far_first))):
            copy.wait_recv()
            onward = vocab_copy(which, out, behind[step - 1], step, core_send, core_recv, partner)
            onward.start()
            passes.append(onward)

    part = pooled.shape[2]
    piece = column_rows.shape[3]
    each = part // piece
    few = column_rows.shape[2]
    kept = {}

    def pool():
        extended[pl.ds(margin, rows), :] = teacher[...]
        starts = spans[0:1, :]
        ends = spans[1:2, :]
        positions = (
            tok * rows - margin + lax.broadcasted_iota(jnp.int32, (rows + 2 * margin, rows), 0)
        )
        inside = (positions >= starts) & (positions < ends)
        member = jnp.where(inside, 1.0, 0.0).astype(jnp.bfloat16)
        ones = jnp.ones((rows + 2 * margin, rows), jnp.bfloat16)
        over_rows = (((0,), (0,)), ((), ()))
        counts = lax.dot_general(member, ones, over_rows, preferred_element_type=jnp.float32)
        for halo in halos:
            halo.wait()
        summed = lax.dot_general(
            member, extended[...], over_rows, preferred_element_type=jnp.float32
        )
        pooled[me] = (summed / counts[:, 0:1]).astype(jnp.bfloat16)
        kept["pooled"] = spread(0, pooled)

    def pass_pooled():
        pass_on(0, pooled, *kept["pooled"])

    def pooled_piece(index):
        start = pl.multiple_of(lax.rem(index, each) * piece, piece)
        first = pl.multiple_of(chip * few, few)
        return pooled.at[lax.div(index, each), pl.ds(first, few), pl.ds(start, piece)]

    def project():
        for onward in kept["pooled"][1]:
            onward.wait()
        total = None
        for j in range(2 * chips):
            term = lax.dot_general(
                proj_weight[:, j * part : (j + 1) * part], pooled[j], (((1,), (1,)), ((), ())),
                preferred_element_type=jnp.float32,
            )
            total = term if total is None else total + term
        projected[me] = total
        kept["projected"] = spread(1, projected)
        pieces = []
        for step in range(1, n_tok):
            pieces.append(
                pltpu.make_async_remote_copy(
                    src_ref=pooled_piece(tok_ahead[step - 1]), dst_ref=column_rows.at[tok, chip],
                    send_sem=tok_send.at[step], recv_sem=tok_recv.at[step],
                    device_id={"tok": tok_ahead[step - 1]}, device_id_type=MESH,
                )
            )
        pieces.append(
            pltpu.make_async_copy(pooled_piece(tok), column_rows.at[tok, chip], keep.at[1])
        )
        for copy in pieces:
            copy.start()
        kept["pieces"] = pieces

    def pass_projected():
        pass_on(1, projected, *kept["projected"])

    def gather_columns():
        for onward in kept["projected"][1]:
            onward.wait()
        for copy in kept["pieces"]:
            copy.wait()
        kept["columns"] = []
        for step in far_first:
            copy = pltpu.make_async_remote_copy(
                src_ref=column_rows.at[:, chip], dst_ref=column_rows.at[:, chip],
                send_sem=row_send.at[step], recv_sem=row_recv.at[step],
                device_id={"vocab": ahead[step - 1]}, device_id_type=MESH,
            )
            copy.start()
            kept["columns"].append(copy)

    jobs = [
        (4.0, pool), (15.0, pass_pooled), (20.0, project), (33.0, pass_projected),
        (40.0, gather_columns),
    ]
    for now, act, name in plan:
        while jobs and jobs[0][0] <= now:
            jobs.pop(0)[1]()
        copy = head_copy(name, act == "send")
        if act == "send":
            copy.start()
            started.append(copy)
        else:
            copy.wait_recv()
    while jobs:
        jobs.pop(0)[1]()
    for copy in kept["columns"]:
        copy.wait()
    for copy in started + kept["pooled"][0] + kept["projected"][0]:
        copy.wait_send()
    own_head.wait()


def front(teacher, spans, proj_weight, head, collective_id):
    n_tok = lax.axis_size("tok")
    n_vocab = lax.axis_size("vocab")
    chips = n_vocab // 2
    rows, part = teacher.shape
    split = rows * 3 // 8 // ROW_TILE * ROW_TILE
    plan = gather_plan(rows, split, SIDE_X, n_tok // SIDE_X)
    moves = len(plan) // 2
    sems = [moves] * 2 + [2] * 2 + [2 * chips] * 4 + [n_tok] * 2 + [chips] * 2 + [2]
    return pl.pallas_call(
        functools.partial(front_kernel, chips, n_tok, plan),
        out_shape=(
            jax.ShapeDtypeStruct((n_tok,) + head.shape, head.dtype),
            jax.ShapeDtypeStruct((n_vocab, rows, part), jnp.bfloat16),
            jax.ShapeDtypeStruct((n_vocab, proj_weight.shape[0], rows), jnp.float32),
            jax.ShapeDtypeStruct(
                (n_tok, chips, rows // chips, part * n_vocab // n_tok), jnp.bfloat16
            ),
        ),
        in_specs=[pl.BlockSpec(memory_space=pltpu.VMEM)] * 4,
        out_specs=[pl.BlockSpec(memory_space=pl.ANY)] + [pl.BlockSpec(memory_space=pltpu.VMEM)] * 3,
        scratch_shapes=[pltpu.VMEM((rows + rows // 2, part), jnp.bfloat16)]
        + [pltpu.SemaphoreType.DMA((size,)) for size in sems],
        compiler_params=pltpu.CompilerParams(collective_id=collective_id, has_side_effects=True),
    )(teacher, spans, proj_weight, head)


def on_device(
    teacher_hidden, span_table, target_ids, student_logits, proj_weight, norm_gain, head_weight
):
    n_tok = lax.axis_size("tok")
    n_vocab = lax.axis_size("vocab")
    rows = teacher_hidden.shape[0]
    width_part = proj_weight.shape[0]
    head_full, _, projected, column_rows = front(
        teacher_hidden, span_table.T, proj_weight, head_weight, 0
    )
    head_full = head_full.reshape(-1, head_weight.shape[1])
    projected_part = lax.dynamic_index_in_dim(
        projected, lax.axis_index("vocab"), 0, keepdims=False
    )
    width = norm_gain.shape[0]
    projected = projected.reshape(width, rows)
    inverse = lax.rsqrt(jnp.sum(projected * projected, axis=0) / width + EPS)
    normed = (projected * inverse[None, :] * norm_gain[:, None]).astype(jnp.bfloat16)

    student = student_logits.astype(jnp.float32)
    head_logits = lax.dot_general(
        normed, head_full, (((0,), (1,)), ((), ())), preferred_element_type=jnp.float32
    )
    vocab_part = student_logits.shape[1]
    vocab_ids = lax.axis_index("vocab") * vocab_part + jnp.arange(vocab_part, dtype=jnp.int32)
    hit = (vocab_ids[None, :] == target_ids[:, None]).astype(jnp.float32)
    student_top = jnp.max(student, axis=1)
    student_exp = jnp.exp(student - student_top[:, None])
    head_top = jnp.max(head_logits, axis=1)
    head_exp = jnp.exp(head_logits - head_top[:, None])
    stats = jnp.stack(
        [
            student_top,
            jnp.sum(student_exp, axis=1),
            jnp.sum(student_exp * (student - head_logits), axis=1),
            jnp.sum(student_exp * head_logits, axis=1),
            head_top,
            jnp.sum(head_exp, axis=1),
            jnp.sum(head_exp * head_logits, axis=1),
            jnp.sum(hit * head_logits, axis=1),
        ]
    )
    merged = vocab_merge(stats, 1)
    student_lse, head_lse, token_loss, inner = (merged[index] for index in range(4))

    prob_student = jnp.exp(student - student_lse[:, None])
    prob_head = jnp.exp(head_logits - head_lse[:, None])
    logit_grad = (2.0 * prob_head - prob_student - hit).astype(jnp.bfloat16)
    grad_parts = lax.dot_general(
        head_full, logit_grad, (((0,), (1,)), ((), ())), preferred_element_type=jnp.float32
    ).astype(jnp.bfloat16)
    gain_part = lax.dynamic_slice_in_dim(
        norm_gain, lax.axis_index("vocab") * width_part, width_part
    )
    scaled_part = projected_part * inverse[None, :]
    out_grads = tail(
        grad_parts.reshape(n_vocab, width_part, rows),
        gain_part[:, None],
        inverse[None, :],
        scaled_part * inner[None, :] / width,
        2,
    )
    proj_grad = lax.dot_general(
        jnp.swapaxes(out_grads, 0, 1).reshape(width_part, n_tok * rows),
        column_rows.reshape(n_tok * rows, -1),
        (((1,), (0,)), ((), ())),
        preferred_element_type=jnp.float32,
    )
    return (token_loss, proj_grad)


def solution(mesh):
    return jax.shard_map(
        on_device,
        mesh=mesh,
        in_specs=(
            P("tok", "vocab"),
            P("tok", None),
            P("tok"),
            P("tok", "vocab"),
            P("vocab", None),
            P(),
            P(("vocab", "tok"), None),
        ),
        out_specs=(P("tok"), P("vocab", "tok")),
        check_vma=False,
    )
```
